512 devices in a mesh: cube: 16 (over x, z_hi, core), tile: 32 (over y, z_lo).
Axes of the slice: x: 4, y: 4, z: 16 (z_hi: 2, z_lo: 8; z = z_hi * 8 + z_lo), core: 2. Of those that a mesh axis runs over, the one named last changes fastest.
Arguments:
- leaf_fronts: float32 [8, 4096, 1, 8192], P(None, 'cube', None, 'tile'), as said below
- middle_fronts: float32 [4, 4096, 1, 8192], P(None, 'cube', None, 'tile'), as said below
- root_front: float32 [2, 4096, 1, 8192], P(None, 'cube', None, 'tile'), as said below
- leaf_scatter: int32 [4, 32, 256], replicated, may hold values from 0 to 255, each once within a row
- middle_scatter: int32 [2, 32, 256], replicated, may hold values from 0 to 255, each once within a row
- leaf_orders: int32 [4], replicated, may hold values from 4096 to 8192, as said below
- middle_orders: int32 [2], replicated, may hold values from 4096 to 8192, as said below
Outputs:
- leaf_panel: bfloat16 [8, 16, 256, 256], P(None, 'cube', 'tile')
- middle_panel: bfloat16 [4, 16, 256, 256], P(None, 'cube', 'tile')
- root_panel: bfloat16 [2, 16, 256, 256], P(None, 'cube', 'tile')
- root_schur: bfloat16 [2, 4096, 1, 8192], P(None, 'cube', None, 'tile')
The draws below stay inside these ranges and needn't reach their ends.
Inputs may be any that keep to these rules, and one draw needn't show every extreme that they name: `leaf_fronts`: each front is symmetric and positive definite. `middle_fronts`: each front is symmetric and positive definite. `root_front`: the front is symmetric and positive definite. `leaf_orders`: some front of the level has all 8192 rows live. `middle_orders`: some front of the level has all 8192 rows live.
All inputs are finite; a program needn't handle non-finite values.
Results may differ from the reference program's by a relative error of at most 0.0052.
Values may be sent and summed in bfloat16 or wider, within the bound.
A program may use at most 64 MiB of HBM per device.

```python
import math
import jax
import jax.numpy as jnp
from jax import lax

PANEL = 256
NTILES = 32
ORDER = 8192
N_CUBE = 16
N_TILE = 32


pivot_diagonal = 8.0


def stored_layout_drawn(natural, fronts):
    groups = N_CUBE // fronts
    rows_per = NTILES // groups
    col_tiles = NTILES // N_TILE
    blocks = natural.reshape(fronts, rows_per, groups, PANEL, col_tiles, N_TILE, PANEL)
    blocks = jnp.transpose(blocks, (1, 0, 2, 3, 4, 5, 6))
    return blocks.reshape(rows_per, N_CUBE * PANEL, col_tiles, N_TILE * PANEL)


def place_pivot(pivot_block, side_block, rest_block, pivot_tile):
    cut_row = pivot_tile * PANEL
    upper_rows = jnp.concatenate([rest_block[:cut_row, :cut_row], side_block[:cut_row], rest_block[:cut_row, cut_row:]], axis=1)
    middle = jnp.concatenate([side_block[:cut_row].T, pivot_block, side_block[cut_row:].T], axis=1)
    lower_rows = jnp.concatenate([rest_block[cut_row:, :cut_row], side_block[cut_row:], rest_block[cut_row:, cut_row:]], axis=1)
    return jnp.concatenate([upper_rows, middle, lower_rows], axis=0)


def coupled_front(key, pivot_tile):
    tri_key, side_key, diag_key = jax.random.split(key, 3)
    rest_rows = ORDER - PANEL
    spread = 0.6 / math.sqrt(PANEL)
    strict_part = jax.random.uniform(tri_key, (PANEL, PANEL), jnp.float32, -spread, spread)
    tile_pos = jnp.arange(PANEL)
    strict_part = jnp.where(tile_pos[:, None] > tile_pos[None, :], strict_part, 0.0)
    leading = jnp.sqrt(1.0 - jnp.sum(strict_part * strict_part, axis=1))
    unit_rows = strict_part + jnp.diag(leading)
    couplings = jnp.clip(jax.random.normal(side_key, (rest_rows, 2 * PANEL), jnp.float32), -4.0, 4.0)
    diag_extra = jnp.exp(jax.random.uniform(diag_key, (rest_rows,), jnp.float32, math.log(0.25), math.log(0.5)))
    couplings = couplings / math.sqrt(PANEL)
    pivot_block = pivot_diagonal * jnp.dot(unit_rows, unit_rows.T, precision=lax.Precision.HIGHEST)
    pivot_block = 0.5 * (pivot_block + pivot_block.T)
    pivot_block = jnp.where(tile_pos[:, None] == tile_pos[None, :], pivot_diagonal, pivot_block)
    side_block = math.sqrt(pivot_diagonal) * jnp.dot(couplings[:, :PANEL], unit_rows.T, precision=lax.Precision.HIGHEST)
    rest_block = jnp.dot(couplings, couplings.T, precision=lax.Precision.HIGHEST)
    rest_block = 0.5 * (rest_block + rest_block.T)
    rest_pos = jnp.arange(rest_rows)
    rest_block = rest_block.at[rest_pos, rest_pos].add(diag_extra)
    return place_pivot(pivot_block, side_block, rest_block, pivot_tile).astype(jnp.float32)


def front_stack(key, fronts, pivot_tile):
    natural = jnp.stack([coupled_front(jax.random.fold_in(key, front_id), pivot_tile) for front_id in range(fronts)])
    return stored_layout_drawn(natural, fronts)


def live_orders(key, fronts):
    low_key, pick_key = jax.random.split(key)
    drawn = jax.random.randint(low_key, (fronts,), ORDER // 2, ORDER + 1, dtype=jnp.int32)
    chosen = jax.random.randint(pick_key, (), 0, fronts, dtype=jnp.int32)
    return jnp.where(jnp.arange(fronts, dtype=jnp.int32) == chosen, ORDER, drawn).astype(jnp.int32)


def draw_leaf_fronts(key, part):
    return front_stack(jax.random.fold_in(key, 11), 4, 0)


def draw_middle_fronts(key, part):
    return front_stack(jax.random.fold_in(key, 12), 2, 1)


def draw_root_front(key, part):
    return front_stack(jax.random.fold_in(key, 13), 1, 2)


def draw_leaf_orders(key, part):
    return live_orders(jax.random.fold_in(key, 21), 4)


def draw_middle_orders(key, part):
    return live_orders(jax.random.fold_in(key, 22), 2)


def setup_inputs(seed: int = 0) -> dict:
    keys = jax.random.split(jax.random.key(seed), 8)
    return {
        "leaf_fronts": draw_leaf_fronts(jax.random.fold_in(keys[7], 71), 0),
        "middle_fronts": draw_middle_fronts(jax.random.fold_in(keys[7], 71), 0),
        "root_front": draw_root_front(jax.random.fold_in(keys[7], 71), 0),
        "leaf_scatter": jax.vmap(lambda own: jax.random.permutation(own, PANEL))(jax.random.split(keys[3], 4 * NTILES)).reshape((4, NTILES, PANEL)).astype(jnp.int32),
        "middle_scatter": jax.vmap(lambda own: jax.random.permutation(own, PANEL))(jax.random.split(keys[4], 2 * NTILES)).reshape((2, NTILES, PANEL)).astype(jnp.int32),
        "leaf_orders": draw_leaf_orders(jax.random.fold_in(keys[7], 71), 0),
        "middle_orders": draw_middle_orders(jax.random.fold_in(keys[7], 71), 0),
    }


def natural_layout(stored, fronts):
    groups = N_CUBE // fronts
    rows_per = NTILES // groups
    col_tiles = NTILES // N_TILE
    blocks = stored.reshape(rows_per, fronts, groups, PANEL, col_tiles, N_TILE, PANEL)
    blocks = jnp.transpose(blocks, (1, 0, 2, 3, 4, 5, 6))
    return blocks.reshape(fronts, ORDER, ORDER)

def stored_layout(natural, fronts):
    groups = N_CUBE // fronts
    rows_per = NTILES // groups
    col_tiles = NTILES // N_TILE
    blocks = natural.reshape(fronts, rows_per, groups, PANEL, col_tiles, N_TILE, PANEL)
    blocks = jnp.transpose(blocks, (1, 0, 2, 3, 4, 5, 6))
    return blocks.reshape(rows_per, N_CUBE * PANEL, col_tiles, N_TILE * PANEL)

def panel_layout(panels, fronts):
    groups = N_CUBE // fronts
    rows_per = NTILES // groups
    blocks = panels.reshape(fronts, rows_per, groups, PANEL, PANEL)
    blocks = jnp.transpose(blocks, (1, 0, 2, 3, 4))
    return blocks.reshape(rows_per, N_CUBE, PANEL, PANEL)

def factor_front(whole, pivot_tile):
    first_row = pivot_tile * PANEL
    corner = whole[first_row:first_row + PANEL, first_row:first_row + PANEL]
    lower_factor = jnp.linalg.cholesky(corner)
    column = whole[:, first_row:first_row + PANEL]
    solved = jax.scipy.linalg.solve_triangular(lower_factor, column.T, lower=True).T
    solved = solved.at[first_row:first_row + PANEL].set(lower_factor)
    factor_panel = solved.astype(jnp.bfloat16)
    zeroed = factor_panel.at[first_row:first_row + PANEL].set(jnp.zeros((PANEL, PANEL), jnp.bfloat16))
    update = jnp.dot(zeroed.astype(jnp.float32), zeroed.T.astype(jnp.float32), preferred_element_type=jnp.float32)
    return (factor_panel, whole - update)

def extend_add(schur_part, live_order, pivot_tile, scatter_rows):
    positions = jnp.arange(ORDER, dtype=jnp.int32)
    keep_rows = ((positions < live_order) & (positions // PANEL != pivot_tile)).astype(jnp.float32)
    masked = schur_part * keep_rows[:, None] * keep_rows[None, :]
    target = positions // PANEL * PANEL + scatter_rows.reshape(-1).astype(jnp.int32)
    rows_done = jnp.zeros((ORDER, ORDER), jnp.float32).at[target].set(masked)
    return jnp.zeros((ORDER, ORDER), jnp.float32).at[:, target].set(rows_done)

def reference(leaf_fronts, middle_fronts, root_front, leaf_scatter, middle_scatter, leaf_orders, middle_orders):
    leaf_natural = natural_layout(leaf_fronts, 4)
    leaf_panels = []
    lifted = []
    for front_id in range(4):
        factor_panel, schur_part = factor_front(leaf_natural[front_id], 0)
        leaf_panels.append(factor_panel)
        lifted.append(extend_add(schur_part, leaf_orders[front_id], 0, leaf_scatter[front_id]))
    middle_natural = natural_layout(middle_fronts, 2)
    middle_panels = []
    raised = []
    for front_id in range(2):
        assembled = middle_natural[front_id] + lifted[2 * front_id] + lifted[2 * front_id + 1]
        factor_panel, schur_part = factor_front(assembled, 1)
        middle_panels.append(factor_panel)
        raised.append(extend_add(schur_part, middle_orders[front_id], 1, middle_scatter[front_id]))
    root_natural = natural_layout(root_front, 1)
    assembled = root_natural[0] + raised[0] + raised[1]
    factor_panel, schur_part = factor_front(assembled, 2)
    return (panel_layout(jnp.stack(leaf_panels), 4), panel_layout(jnp.stack(middle_panels), 2), panel_layout(factor_panel[None], 1), stored_layout(schur_part[None], 1).astype(jnp.bfloat16))
```

```python
import jax
import jax.numpy as jnp
from jax import lax
from jax.experimental import pallas as pl
from jax.experimental.pallas import tpu as pltpu
from jax.sharding import PartitionSpec as P

MESH = pl.DeviceIdType.MESH
HIGHEST = lax.Precision.HIGHEST
F32, BF16 = jnp.float32, jnp.bfloat16
W = 256


def dot(a, b, ca, cb, precision=None):
    return lax.dot_general(
        a, b, (((ca,), (cb,)), ((), ())), precision=precision, preferred_element_type=F32
    )


def inverse_factor_128(a):
    n = a.shape[0]
    rows = lax.broadcasted_iota(jnp.int32, (n, 1), 0)
    first = lax.broadcasted_iota(jnp.int32, (8, 1), 0)
    eye = lax.broadcasted_iota(jnp.int32, (n, n), 0) == lax.broadcasted_iota(jnp.int32, (n, n), 1)

    def trip(block, ab):
        a, b = ab
        live = rows < n - 8 * block
        pivots = jnp.ones((8, 1), F32)
        for i in range(8):
            row_a, row_b = a[i : i + 1, :], b[i : i + 1, :]
            pivot = a[i : i + 1, i : i + 1]
            pivots = jnp.where(first == i, pivot, pivots)
            scale = jnp.where(live & (rows > i), a[:, i : i + 1] * (1.0 / pivot), 0.0)
            a = a - scale * row_a
            b = b - scale * row_b
        b = jnp.concatenate([b[8:], b[:8] * lax.rsqrt(pivots)], 0)
        a = pltpu.roll(jnp.concatenate([a[8:], a[:8]], 0), n - 8, 1)
        return a, b

    return lax.fori_loop(0, n // 8, trip, (a, eye.astype(F32)))[1]


def inverse_factor(source, target):
    h = W // 2
    i11 = inverse_factor_128(source[:h, :h])
    l21 = dot(source[h:, :h], i11, 1, 1, HIGHEST)
    i22 = inverse_factor_128(source[h:, h:] - dot(l21, l21, 1, 1, HIGHEST))
    i21 = -dot(i22, dot(l21, i11, 1, 0, HIGHEST), 1, 0, HIGHEST)
    target[:h, :h] = i11
    target[:h, h:] = jnp.zeros((h, h), F32)
    target[h:, :h] = i21
    target[h:, h:] = i22


def solve_panel(row_block, inverse):
    return dot(row_block, inverse, 0, 1, HIGHEST)


def place(left, block, right):
    high = block.astype(BF16)
    low = (block - high.astype(F32)).astype(BF16)
    total = None
    for part in (high, low):
        moved = dot(left, part, 1, 0).astype(BF16)
        moved = dot(moved, right, 1, 1)
        total = moved if total is None else total + moved
    return total


def kernel(
    a2, a1, a0, s2, s1, o2, o1,
    leaf_out, mid_out, root_out, schur_out,
    ta2, ta1, pa, cb, rb, li, yb, l1i, l0i, hs, pl2, pm1, acc, ts, psend, precv, msend, mrecv,
    send_sem, r_ta2, r_ta1, r_pa, r_cb, r_rb, r_li, r_yb, r_l1, r_l0, r_ps, r_ms,
):
    cube, t = lax.axis_index("cube"), lax.axis_index("tile")
    x, zh, c = cube // 4, (cube // 2) % 2, cube % 2
    y, zl = t // 8, t % 8
    g = 2 * zh + c
    mover = c == zh
    pending = []

    def dev(x_, zh_, c_, y_, zl_):
        return (x_ * 4 + zh_ * 2 + c_, y_ * 8 + zl_)

    def send(pred, src, dst, recv, target):
        index = len(pending)

        def make():
            return pltpu.make_async_remote_copy(
                src_ref=src, dst_ref=dst, send_sem=send_sem.at[index], recv_sem=recv,
                device_id=target(), device_id_type=MESH,
            )

        pending.append((pred, make))

        @pl.when(pred)
        def _():
            make().start()

    def arrive(pred, dst, recv):
        @pl.when(pred)
        def _():
            pltpu.make_async_remote_copy(
                src_ref=dst, dst_ref=dst, send_sem=send_sem.at[0], recv_sem=recv,
                device_id=(cube, t), device_id_type=MESH,
            ).wait_recv()

    always = x >= 0
    is_pd0 = (zh == 0) & (c == 0)
    is_pd1 = (zh == 0) & (c == 1) & (x % 2 == 0)
    is_pd2 = (x == 0) & (zh == 1) & (c == 0)

    send((zh == 0) & (c == 1) & (x % 2 == 1), a2.at[0], pa, r_pa, lambda: dev(x - 1, zh, c, y, zl))
    for apart in (1, 3, 2):
        xd = (x + apart) % 4
        for r in range(2):
            send(always, a2.at[4 * r + xd], ta2.at[x, r], r_ta2.at[x, r], lambda xd=xd: dev(xd, zh, c, y, zl))
    xo = (x + 2) % 4
    for r in range(2):
        send(always, a1.at[2 * r + xo // 2], ta1.at[x // 2, r], r_ta1.at[x // 2, r], lambda: dev(xo, zh, c, y, zl))
    for r in range(2):
        ta2[x, r] = a2[4 * r + x]
        ta1[x // 2, r] = a1[2 * r + x // 2]

    slot = lax.broadcasted_iota(jnp.int32, (W, W), 0)
    offset = lax.broadcasted_iota(jnp.int32, (1, W), 1)

    def mover_matrix(table, orders, front, tile, pivot):
        keep = (tile * W + offset < orders[front]) & (tile != pivot)
        hit = (table[front, pl.ds(tile, 1), :] == slot) & keep
        return jnp.where(hit, 1.0, 0.0).astype(BF16)

    row_tiles = (4 * x + g, 4 * x + g + 16)

    @pl.loop(0, 4)
    def _(l):
        for w, tile in enumerate(row_tiles + (t,)):
            pl2[l, w] = mover_matrix(s2, o2, l, tile, 0)

    @pl.loop(0, 2)
    def _(m):
        for w, tile in enumerate(row_tiles + (t,)):
            pm1[m, w] = mover_matrix(s1, o1, m, tile, 1)

    lower = lax.broadcasted_iota(jnp.int32, (W, W), 0) >= lax.broadcasted_iota(jnp.int32, (W, W), 1)

    def fan_out(who, ref, recv, root_zl, ch):
        for other in range(8):
            if other != root_zl:
                send(who & (y == 0) & (zl == root_zl), ref, ref, recv, lambda o=other: dev(x, 0, ch, 0, o))
        arrive(who & ((y != 0) | (zl != root_zl)), ref, recv)
        for other in (1, 3, 2):
            send(who & (y == 0), ref, ref, recv, lambda o=other: dev(x, 0, ch, o, zl))

    @pl.when(is_pd0 & (t == 0))
    def _():
        inverse_factor(a2.at[0], li)

    fan_out(is_pd0, li, r_li, 0, 0)

    @pl.when(is_pd0)
    def _():
        panel = solve_panel(a2[0], li[...])
        cb[x] = jnp.where(lower | (t != 0), panel, 0.0).astype(BF16)

    def column_stage(k, holder, own, known):
        arrive(mover & jnp.logical_not(own), cb.at[k], r_cb.at[k])
        send(mover & jnp.logical_not(known), cb.at[k], cb.at[k], r_cb.at[k], lambda: dev(x, zh, 1 - c, y, zl))
        for apart in (1, 3, 2):
            send(mover & holder, cb.at[k], cb.at[k], r_cb.at[k], lambda a=apart: dev((x + a) % 4, zh, c, y, zl))

    def row_stage(k):
        z0 = 4 * (x % 2) + 2 * zh
        for cc in range(2):
            for r in range(2):
                line = mover & (y == x // 2 + 2 * r)
                at = z0 + cc
                source = line & (zl == at)
                ref, recv = rb.at[k, r, cc], r_rb.at[k, r, cc]

                @pl.when(source)
                def _():
                    rb[k, r, cc] = cb[k]

                arrive(mover & jnp.logical_not(source), ref, recv)
                send(line & (zl >= at) & (zl < 7), ref, ref, recv, lambda: dev(x, zh, c, y, zl + 1))
                send(line & (zl <= at) & (zl > 0), ref, ref, recv, lambda: dev(x, zh, c, y, zl - 1))
                for apart in (1, 3, 2):
                    send(line, ref, ref, recv, lambda a=apart: dev(x, zh, c, (y + a) % 4, zl))
                send(mover & (c != cc), ref, ref, recv, lambda: dev(x, zh, 1 - c, y, zl))

    for l in range(4):
        send(is_pd0 & (x == l), cb.at[l], cb.at[l], r_cb.at[l], lambda: dev(x, 1, 1, y, zl))
    for l in range(4):
        column_stage(l, x == l, is_pd0 & (x == l), always & False)
    for l in range(4):
        arrive(jnp.logical_not(mover), cb.at[l], r_cb.at[l])

    arrive(is_pd1, pa, r_pa)

    @pl.when(is_pd1)
    def _():
        total = a1[0]
        for i in range(2):
            block = a2[0] if i == 0 else pa[...]
            left = mover_matrix(s2, o2, x + i, 1, 0)
            total = total + place(left, block, pl2[x + i, 2])
        hs[...] = total

        @pl.when(t == 1)
        def _():
            for i in range(2):
                yb[i] = dot(pl2[x + i, 2], cb[x + i], 1, 0).astype(BF16)

    fan_out(is_pd1, yb, r_yb, 1, 1)

    @pl.when(is_pd1)
    def _():
        total = hs[...]
        for i in range(2):
            mine = dot(pl2[x + i, 2], cb[x + i], 1, 0).astype(BF16)
            total = total - dot(yb[i], mine, 1, 1)
        hs[...] = total

        @pl.when(t == 1)
        def _():
            inverse_factor(hs, l1i)

    fan_out(is_pd1, l1i, r_l1, 1, 1)

    @pl.when(is_pd1)
    def _():
        panel = solve_panel(hs[...], l1i[...])
        cb[4 + x // 2] = jnp.where(lower | (t != 1), panel, 0.0).astype(BF16)

    for m in range(2):
        mine = is_pd1 & (x == 2 * m)
        send(mine, cb.at[4 + m], cb.at[4 + m], r_cb.at[4 + m], lambda: dev(x, 0, 0, y, zl))
        send(mine, cb.at[4 + m], cb.at[4 + m], r_cb.at[4 + m], lambda: dev(x, 1, 1, y, zl))

    for l in range(4):
        row_stage(l)

    for l in range(4):
        for r in range(2):
            arrive(x != l, ta2.at[l, r], r_ta2.at[l, r])
    for m in range(2):
        for r in range(2):
            arrive(x // 2 != m, ta1.at[m, r], r_ta1.at[m, r])

    for r in range(2):
        ts[0] = ta1[0, r]
        ts[1] = ta1[1, r]

        @pl.loop(0, 4)
        def _(l):
            ts[l // 2] += place(pl2[l, r], ta2[l, r], pl2[l, 2])

        acc[r] = a0[r]

        @pl.loop(0, 2)
        def _(m):
            acc[r] += place(pm1[m, r], ts[m], pm1[m, 2])

    def carried(m, w, block):
        return dot(pm1[m, w], block, 1, 0).astype(BF16)

    for l in range(4):
        for r in range(2):
            arrive(jnp.logical_not(mover), rb.at[l, r, c], r_rb.at[l, r, c])

    pick = (
        lax.broadcasted_iota(jnp.int32, (8, W), 0) + 8 * t == lax.broadcasted_iota(jnp.int32, (8, W), 1)
    )
    pick = jnp.where(pick, 1.0, 0.0).astype(BF16)

    @pl.loop(0, 4)
    def _(l):
        m = l // 2
        col = carried(m, 2, dot(pl2[l, 2], cb[l], 1, 0).astype(BF16))
        for r in range(2):
            psend[l, r] = dot(pick, rb[l, r, c], 1, 0)
            row = carried(m, r, dot(pl2[l, r], rb[l, r, c], 1, 0).astype(BF16))
            acc[r] -= dot(row, col, 1, 1)

    for apart in (1, 3, 2):
        xd = (x + apart) % 4
        send(always, psend.at[xd], precv.at[x], r_ps.at[x], lambda xd=xd: dev(xd, zh, c, y, zl))
    precv[x] = psend[x]

    for m in range(2):
        column_stage(4 + m, x == 2 * m, always & False, (zh == 0) & (x == 2 * m))
    for m in range(2):
        arrive(jnp.logical_not(mover) & jnp.logical_not(is_pd1 & (x == 2 * m)), cb.at[4 + m], r_cb.at[4 + m])
    for m in range(2):
        row_stage(4 + m)
    for m in range(2):
        for r in range(2):
            arrive(jnp.logical_not(mover), rb.at[4 + m, r, c], r_rb.at[4 + m, r, c])

    @pl.loop(0, 2)
    def _(m):
        col = carried(m, 2, cb[4 + m])
        for r in range(2):
            msend[m, r] = dot(pick, rb[4 + m, r, c], 1, 0)
            acc[r] -= dot(carried(m, r, rb[4 + m, r, c]), col, 1, 1)

    send(always, msend.at[xo // 2], mrecv.at[x // 2], r_ms.at[x // 2], lambda: dev(xo, zh, c, y, zl))
    mrecv[x // 2] = msend[x // 2]

    @pl.when(is_pd2)
    def _():
        high = acc[0].astype(BF16)
        cb[6] = high
        cb[7] = (acc[0] - high.astype(F32)).astype(BF16)

    for k in (6, 7):
        send(is_pd2, cb.at[k], cb.at[k], r_cb.at[k], lambda: dev(0, 1, 1, y, zl))
        send(is_pd2, cb.at[k], cb.at[k], r_cb.at[k], lambda: dev(0, 0, 0, y, zl))

    @pl.when(is_pd2 & (t == 2))
    def _():
        inverse_factor(acc.at[0], l0i)

    root = is_pd2 & (t == 2)
    send(root, l0i, l0i, r_l0, lambda: dev(0, 1, 1, 0, 2))

    for k in (6, 7):
        column_stage(k, x == 0, always & False, (zh == 1) & (x == 0))
    for k in (6, 7):
        row_stage(k)
    for k in (6, 7):
        arrive(jnp.logical_not(mover) & jnp.logical_not(is_pd2), cb.at[k], r_cb.at[k])
        for r in range(2):
            arrive(jnp.logical_not(mover), rb.at[k, r, c], r_rb.at[k, r, c])

    arrive(jnp.logical_not(root), l0i, r_l0)
    two = mover & (y == 0) & (zl == 2)
    send(two & (x == 0) & (zh == 1), l0i, l0i, r_l0, lambda: dev(0, 0, 0, 0, 2))
    for other in (1, 3, 2):
        send(two & (x == 0), l0i, l0i, r_l0, lambda o=other: dev(o, zh, c, 0, 2))
    for other in (1, 3, 2):
        send(two, l0i, l0i, r_l0, lambda o=other: dev(x, zh, c, o, 2))
    for other in (3, 1, 4, 0, 5, 6, 7):
        send(mover & (zl == 2), l0i, l0i, r_l0, lambda o=other: dev(x, zh, c, y, o))
    send(
        mover & jnp.logical_not((x == 0) & (zh == 1) & (t == 2)),
        l0i, l0i, r_l0, lambda: dev(x, zh, 1 - c, y, zl),
    )

    def last_panel(high, low):
        return solve_panel(high.astype(F32) + low.astype(F32), l0i[...])

    col = last_panel(cb[6], cb[7])
    col = jnp.where(t == 2, 0.0, col).astype(BF16)
    for r in range(2):
        tile = row_tiles[r]
        full = last_panel(rb[6, r, c], rb[7, r, c])
        full = jnp.where(lower | (tile != 2), full, 0.0).astype(BF16)
        root_out[r, 0] = dot(pick, full, 1, 0).astype(BF16)
        row = jnp.where(tile == 2, jnp.zeros_like(full), full)
        schur_out[r, :, 0, :] = (acc[r] - dot(row, col, 1, 1)).astype(BF16)

    for s in range(4):
        arrive(x != s, precv.at[s], r_ps.at[s])
    for s in range(2):
        arrive(x // 2 != s, mrecv.at[s], r_ms.at[s])
    for s in range(4):
        for r in range(2):
            leaf_out[4 * r + s, 0] = precv[s, r].astype(BF16)
    for s in range(2):
        for r in range(2):
            mid_out[2 * r + s, 0] = mrecv[s, r].astype(BF16)

    for pred, make in pending:

        @pl.when(pred)
        def _(make=make):
            make().wait_send()


def per_device(leaf, middle, root, s2, s1, o2, o1):
    vmem = pl.BlockSpec(memory_space=pltpu.VMEM)
    smem = pl.BlockSpec(memory_space=pltpu.SMEM)
    dma = pltpu.SemaphoreType.DMA
    outs = [
        jax.ShapeDtypeStruct((8, 1, 8, W), BF16),
        jax.ShapeDtypeStruct((4, 1, 8, W), BF16),
        jax.ShapeDtypeStruct((2, 1, 8, W), BF16),
        jax.ShapeDtypeStruct((2, W, 1, W), BF16),
    ]
    tile = (W, W)
    scratch = [
        pltpu.VMEM((4, 2) + tile, F32),
        pltpu.VMEM((2, 2) + tile, F32),
        pltpu.VMEM(tile, F32),
        pltpu.VMEM((8,) + tile, BF16),
        pltpu.VMEM((8, 2, 2) + tile, BF16),
        pltpu.VMEM(tile, F32),
        pltpu.VMEM((2,) + tile, BF16),
        pltpu.VMEM(tile, F32),
        pltpu.VMEM(tile, F32),
        pltpu.VMEM(tile, F32),
        pltpu.VMEM((4, 3) + tile, BF16),
        pltpu.VMEM((2, 3) + tile, BF16),
        pltpu.VMEM((2,) + tile, F32),
        pltpu.VMEM((2,) + tile, F32),
        pltpu.VMEM((4, 2, 8, W), F32),
        pltpu.VMEM((4, 2, 8, W), F32),
        pltpu.VMEM((2, 2, 8, W), F32),
        pltpu.VMEM((2, 2, 8, W), F32),
        dma((SENDS,)),
        dma((4, 2)), dma((2, 2)), dma, dma((8,)), dma((8, 2, 2)),
        dma, dma, dma, dma, dma((4,)), dma((2,)),
    ]
    return pl.pallas_call(
        kernel,
        out_shape=outs,
        in_specs=[vmem] * 5 + [smem] * 2,
        out_specs=[vmem] * 4,
        scratch_shapes=scratch,
        compiler_params=pltpu.CompilerParams(has_side_effects=True, vmem_limit_bytes=60 * 2**20),
        name="window",
    )(leaf.reshape(8, W, W), middle.reshape(4, W, W), root.reshape(2, W, W), s2, s1, o2, o1)


SENDS = 360


def solution(mesh):
    return jax.shard_map(
        per_device,
        mesh=mesh,
        in_specs=(P(None, "cube", None, "tile"),) * 3 + (P(),) * 4,
        out_specs=(P(None, "cube", "tile", None),) * 3 + (P(None, "cube", None, "tile"),),
        check_vma=False,
    )
```

```python
import jax
import jax.numpy as jnp
from jax import lax
from jax.experimental import pallas as pl
from jax.experimental.pallas import tpu as pltpu
from jax.sharding import PartitionSpec as P

MESH = pl.DeviceIdType.MESH
HIGHEST = lax.Precision.HIGHEST
F32, BF16 = jnp.float32, jnp.bfloat16
W = 256


def dot(a, b, ca, cb, precision=None):
    return lax.dot_general(
        a, b, (((ca,), (cb,)), ((), ())), precision=precision, preferred_element_type=F32
    )


def inverse_factor_128(a):
    n = a.shape[0]
    rows = lax.broadcasted_iota(jnp.int32, (n, 1), 0)
    first = lax.broadcasted_iota(jnp.int32, (8, 1), 0)
    eye = lax.broadcasted_iota(jnp.int32, (n, n), 0) == lax.broadcasted_iota(jnp.int32, (n, n), 1)

    def trip(block, ab):
        a, b = ab
        live = rows < n - 8 * block
        pivots = jnp.ones((8, 1), F32)
        for i in range(8):
            row_a, row_b = a[i : i + 1, :], b[i : i + 1, :]
            pivot = a[i : i + 1, i : i + 1]
            pivots = jnp.where(first == i, pivot, pivots)
            scale = jnp.where(live & (rows > i), a[:, i : i + 1] * (1.0 / pivot), 0.0)
            a = a - scale * row_a
            b = b - scale * row_b
        b = jnp.concatenate([b[8:], b[:8] * lax.rsqrt(pivots)], 0)
        a = pltpu.roll(jnp.concatenate([a[8:], a[:8]], 0), n - 8, 1)
        return a, b

    return lax.fori_loop(0, n // 8, trip, (a, eye.astype(F32)))[1]


def inverse_factor(source, target):
    h = W // 2
    i11 = inverse_factor_128(source[:h, :h])
    l21 = dot(source[h:, :h], i11, 1, 1, HIGHEST)
    i22 = inverse_factor_128(source[h:, h:] - dot(l21, l21, 1, 1, HIGHEST))
    i21 = -dot(i22, dot(l21, i11, 1, 0, HIGHEST), 1, 0, HIGHEST)
    target[:h, :h] = i11
    target[:h, h:] = jnp.zeros((h, h), F32)
    target[h:, :h] = i21
    target[h:, h:] = i22


def solve_panel(row_block, inverse):
    return dot(row_block, inverse, 0, 1, HIGHEST)


def place(left, block, right):
    high = block.astype(BF16)
    low = (block - high.astype(F32)).astype(BF16)
    total = None
    for part in (high, low):
        moved = dot(left, part, 1, 0).astype(BF16)
        moved = dot(moved, right, 1, 1)
        total = moved if total is None else total + moved
    return total


def kernel(
    a2, a1, a0, s2, s1, o2, o1,
    leaf_out, mid_out, root_out, schur_out,
    ta2, ta1, pa, cb, rb, li, yb, l1i, l0i, hs, pl2, pm1, acc, ts, psend, precv, msend, mrecv,
    send_sem, r_ta2, r_ta1, r_pa, r_cb, r_rb, r_li, r_yb, r_l1, r_l0, r_ps, r_ms,
):
    cube, t = lax.axis_index("cube"), lax.axis_index("tile")
    x, zh, c = cube // 4, (cube // 2) % 2, cube % 2
    y, zl = t // 8, t % 8
    g = 2 * zh + c
    mover = c == zh
    pending = []

    def dev(x_, zh_, c_, y_, zl_):
        return (x_ * 4 + zh_ * 2 + c_, y_ * 8 + zl_)

    def send(pred, src, dst, recv, target):
        index = len(pending)

        def make():
            return pltpu.make_async_remote_copy(
                src_ref=src, dst_ref=dst, send_sem=send_sem.at[index], recv_sem=recv,
                device_id=target(), device_id_type=MESH,
            )

        assert index < SENDS
        pending.append((pred, make))

        @pl.when(pred)
        def _():
            make().start()

    def arrive(pred, dst, recv):
        @pl.when(pred)
        def _():
            pltpu.make_async_remote_copy(
                src_ref=dst, dst_ref=dst, send_sem=send_sem.at[0], recv_sem=recv,
                device_id=(cube, t), device_id_type=MESH,
            ).wait_recv()

    always = x >= 0
    is_pd0 = (zh == 0) & (c == 0)
    is_pd1 = (zh == 0) & (c == 1) & (x % 2 == 0)
    is_pd2 = (x == 0) & (zh == 1) & (c == 0)

    send((zh == 0) & (c == 1) & (x % 2 == 1), a2.at[0], pa, r_pa, lambda: dev(x - 1, zh, c, y, zl))
    for apart in (1, 3, 2):
        xd = (x + apart) % 4
        for r in range(2):
            send(always, a2.at[4 * r + xd], ta2.at[x, r], r_ta2.at[x, r], lambda xd=xd: dev(xd, zh, c, y, zl))
    xo = (x + 2) % 4
    for r in range(2):
        send(always, a1.at[2 * r + xo // 2], ta1.at[x // 2, r], r_ta1.at[x // 2, r], lambda: dev(xo, zh, c, y, zl))
    for r in range(2):
        ta2[x, r] = a2[4 * r + x]
        ta1[x // 2, r] = a1[2 * r + x // 2]

    slot = lax.broadcasted_iota(jnp.int32, (W, W), 0)
    offset = lax.broadcasted_iota(jnp.int32, (1, W), 1)

    def mover_matrix(table, orders, front, tile, pivot):
        keep = (tile * W + offset < orders[front]) & (tile != pivot)
        hit = (table[front, pl.ds(tile, 1), :] == slot) & keep
        return jnp.where(hit, 1.0, 0.0).astype(BF16)

    row_tiles = (4 * x + g, 4 * x + g + 16)

    @pl.loop(0, 4)
    def _(l):
        for w, tile in enumerate(row_tiles + (t,)):
            pl2[l, w] = mover_matrix(s2, o2, l, tile, 0)

    @pl.loop(0, 2)
    def _(m):
        for w, tile in enumerate(row_tiles + (t,)):
            pm1[m, w] = mover_matrix(s1, o1, m, tile, 1)

    lower = lax.broadcasted_iota(jnp.int32, (W, W), 0) >= lax.broadcasted_iota(jnp.int32, (W, W), 1)

    half = W // 2

    def pieces(ref, recv):
        return (
            (ref.at[:half, :half], recv.at[0]),
            (ref.at[half : half + half // 2], recv.at[1]),
            (ref.at[half + half // 2 :], recv.at[2]),
        )

    def clear_upper(ref):
        ref[:half, half:] = jnp.zeros((half, half), F32)

    def fan_out(who, ref, recv, root_zl, ch):
        for other in range(8):
            if other != root_zl:
                send(who & (y == 0) & (zl == root_zl), ref, ref, recv, lambda o=other: dev(x, 0, ch, 0, o))
        arrive(who & ((y != 0) | (zl != root_zl)), ref, recv)
        for other in (1, 3, 2):
            send(who & (y == 0), ref, ref, recv, lambda o=other: dev(x, 0, ch, o, zl))

    @pl.when(is_pd0 & (t == 0))
    def _():
        inverse_factor(a2.at[0], li)

    @pl.when(jnp.logical_not(is_pd0 & (t == 0)))
    def _():
        clear_upper(li)

    for part, recv in pieces(li, r_li):
        fan_out(is_pd0, part, recv, 0, 0)

    @pl.when(is_pd0)
    def _():
        panel = solve_panel(a2[0], li[...])
        cb[x] = jnp.where(lower | (t != 0), panel, 0.0).astype(BF16)

    def column_stage(k, holder, own, known):
        arrive(mover & jnp.logical_not(own), cb.at[k], r_cb.at[k])
        send(mover & jnp.logical_not(known), cb.at[k], cb.at[k], r_cb.at[k], lambda: dev(x, zh, 1 - c, y, zl))
        for apart in (1, 3, 2):
            send(mover & holder, cb.at[k], cb.at[k], r_cb.at[k], lambda a=apart: dev((x + a) % 4, zh, c, y, zl))

    def line(r):
        return mover & (y == x // 2 + 2 * r)

    def row_stage(k):
        z0 = 4 * (x % 2) + 2 * zh
        for cc in range(2):
            for r in range(2):
                at = z0 + cc
                source = line(r) & (zl == at)
                ref, recv = rb.at[k, r, cc], r_rb.at[k, r, cc]

                @pl.when(source)
                def _():
                    rb[k, r, cc] = cb[k]

                arrive(line(r) & (zl != at), ref, recv)
                send(line(r) & (zl >= at) & (zl < 7), ref, ref, recv, lambda: dev(x, zh, c, y, zl + 1))
                send(line(r) & (zl <= at) & (zl > 0), ref, ref, recv, lambda: dev(x, zh, c, y, zl - 1))
                for apart in (1, 3, 2):
                    send(line(r), ref, ref, recv, lambda a=apart, cc=cc: dev(x, zh, cc, (y + a) % 4, zl))
                send(line(r) & (c != cc), ref, ref, recv, lambda: dev(x, zh, 1 - c, y, zl))

    def rows_here(k):
        for r in range(2):
            arrive(jnp.logical_not(line(r)), rb.at[k, r, c], r_rb.at[k, r, c])

    for l in range(4):
        send(is_pd0 & (x == l), cb.at[l], cb.at[l], r_cb.at[l], lambda: dev(x, 1, 1, y, zl))
    for l in range(4):
        column_stage(l, x == l, is_pd0 & (x == l), always & False)
    for l in range(4):
        arrive(jnp.logical_not(mover), cb.at[l], r_cb.at[l])

    arrive(is_pd1, pa, r_pa)

    @pl.when(is_pd1)
    def _():
        total = a1[0]
        for i in range(2):
            block = a2[0] if i == 0 else pa[...]
            left = mover_matrix(s2, o2, x + i, 1, 0)
            total = total + place(left, block, pl2[x + i, 2])
        hs[...] = total

        @pl.when(t == 1)
        def _():
            for i in range(2):
                yb[i] = dot(pl2[x + i, 2], cb[x + i], 1, 0).astype(BF16)

    fan_out(is_pd1, yb, r_yb, 1, 1)

    @pl.when(is_pd1)
    def _():
        total = hs[...]
        for i in range(2):
            mine = dot(pl2[x + i, 2], cb[x + i], 1, 0).astype(BF16)
            total = total - dot(yb[i], mine, 1, 1)
        hs[...] = total

        @pl.when(t == 1)
        def _():
            inverse_factor(hs, l1i)

    @pl.when(jnp.logical_not(is_pd1 & (t == 1)))
    def _():
        clear_upper(l1i)

    for part, recv in pieces(l1i, r_l1):
        fan_out(is_pd1, part, recv, 1, 1)

    @pl.when(is_pd1)
    def _():
        panel = solve_panel(hs[...], l1i[...])
        cb[4 + x // 2] = jnp.where(lower | (t != 1), panel, 0.0).astype(BF16)

    for m in range(2):
        mine = is_pd1 & (x == 2 * m)
        send(mine, cb.at[4 + m], cb.at[4 + m], r_cb.at[4 + m], lambda: dev(x, 0, 0, y, zl))
        send(mine, cb.at[4 + m], cb.at[4 + m], r_cb.at[4 + m], lambda: dev(x, 1, 1, y, zl))

    for l in range(4):
        row_stage(l)

    for l in range(4):
        for r in range(2):
            arrive(x != l, ta2.at[l, r], r_ta2.at[l, r])
    for m in range(2):
        for r in range(2):
            arrive(x // 2 != m, ta1.at[m, r], r_ta1.at[m, r])

    for r in range(2):
        ts[0] = ta1[0, r]
        ts[1] = ta1[1, r]

        @pl.loop(0, 4)
        def _(l):
            ts[l // 2] += place(pl2[l, r], ta2[l, r], pl2[l, 2])

        acc[r] = a0[r]

        @pl.loop(0, 2)
        def _(m):
            acc[r] += place(pm1[m, r], ts[m], pm1[m, 2])

    def carried(m, w, block):
        return dot(pm1[m, w], block, 1, 0).astype(BF16)

    for m in range(2):
        column_stage(4 + m, x == 2 * m, always & False, (zh == 0) & (x == 2 * m))
    for m in range(2):
        arrive(jnp.logical_not(mover) & jnp.logical_not(is_pd1 & (x == 2 * m)), cb.at[4 + m], r_cb.at[4 + m])
    for m in range(2):
        row_stage(4 + m)
    for k in range(6):
        rows_here(k)

    pick = (
        lax.broadcasted_iota(jnp.int32, (8, W), 0) + 8 * t == lax.broadcasted_iota(jnp.int32, (8, W), 1)
    )
    pick = jnp.where(pick, 1.0, 0.0).astype(BF16)

    @pl.loop(0, 4)
    def _(l):
        m = l // 2
        col = carried(m, 2, dot(pl2[l, 2], cb[l], 1, 0).astype(BF16))
        for r in range(2):
            psend[l, r] = dot(pick, rb[l, r, c], 1, 0)
            row = carried(m, r, dot(pl2[l, r], rb[l, r, c], 1, 0).astype(BF16))
            acc[r] -= dot(row, col, 1, 1)

    for apart in (1, 3, 2):
        xd = (x + apart) % 4
        send(always, psend.at[xd], precv.at[x], r_ps.at[x], lambda xd=xd: dev(xd, zh, c, y, zl))
    precv[x] = psend[x]

    @pl.loop(0, 2)
    def _(m):
        col = carried(m, 2, cb[4 + m])
        for r in range(2):
            msend[m, r] = dot(pick, rb[4 + m, r, c], 1, 0)
            acc[r] -= dot(carried(m, r, rb[4 + m, r, c]), col, 1, 1)

    send(always, msend.at[xo // 2], mrecv.at[x // 2], r_ms.at[x // 2], lambda: dev(xo, zh, c, y, zl))
    mrecv[x // 2] = msend[x // 2]

    @pl.when(is_pd2)
    def _():
        high = acc[0].astype(BF16)
        cb[6] = high
        cb[7] = (acc[0] - high.astype(F32)).astype(BF16)

    for k in (6, 7):
        send(is_pd2, cb.at[k], cb.at[k], r_cb.at[k], lambda: dev(0, 1, 1, y, zl))
        send(is_pd2, cb.at[k], cb.at[k], r_cb.at[k], lambda: dev(0, 0, 0, y, zl))

    @pl.when(is_pd2 & (t == 2))
    def _():
        inverse_factor(acc.at[0], l0i)

    root = is_pd2 & (t == 2)

    @pl.when(jnp.logical_not(root))
    def _():
        clear_upper(l0i)

    for part, recv in pieces(l0i, r_l0):
        send(root, part, part, recv, lambda: dev(0, 1, 1, 0, 2))

    for k in (6, 7):
        column_stage(k, x == 0, always & False, (zh == 1) & (x == 0))
    for k in (6, 7):
        row_stage(k)
    for k in (6, 7):
        arrive(jnp.logical_not(mover) & jnp.logical_not(is_pd2), cb.at[k], r_cb.at[k])
        rows_here(k)

    two = mover & (y == 0) & (zl == 2)
    for part, recv in pieces(l0i, r_l0):
        arrive(jnp.logical_not(root), part, recv)
        send(two & (x == 0) & (zh == 1), part, part, recv, lambda: dev(0, 0, 0, 0, 2))
        for other in (1, 3, 2):
            send(two & (x == 0), part, part, recv, lambda o=other: dev(o, zh, c, 0, 2))
        for other in (1, 3, 2):
            send(two, part, part, recv, lambda o=other: dev(x, zh, c, o, 2))
        for at, other in ((2, 5), (2, 3), (2, 1), (5, 7), (5, 6), (3, 4), (1, 0)):
            send(mover & (zl == at), part, part, recv, lambda o=other: dev(x, zh, c, y, o))
        send(
            mover & jnp.logical_not((x == 0) & (zh == 1) & (t == 2)),
            part, part, recv, lambda: dev(x, zh, 1 - c, y, zl),
        )

    def last_panel(high, low):
        return solve_panel(high.astype(F32) + low.astype(F32), l0i[...])

    col = last_panel(cb[6], cb[7])
    col = jnp.where(t == 2, 0.0, col).astype(BF16)
    for r in range(2):
        tile = row_tiles[r]
        full = last_panel(rb[6, r, c], rb[7, r, c])
        full = jnp.where(lower | (tile != 2), full, 0.0).astype(BF16)
        root_out[r, 0] = dot(pick, full, 1, 0).astype(BF16)
        row = jnp.where(tile == 2, jnp.zeros_like(full), full)
        schur_out[r, :, 0, :] = (acc[r] - dot(row, col, 1, 1)).astype(BF16)

    for s in range(4):
        arrive(x != s, precv.at[s], r_ps.at[s])
    for s in range(2):
        arrive(x // 2 != s, mrecv.at[s], r_ms.at[s])
    for s in range(4):
        for r in range(2):
            leaf_out[4 * r + s, 0] = precv[s, r].astype(BF16)
    for s in range(2):
        for r in range(2):
            mid_out[2 * r + s, 0] = mrecv[s, r].astype(BF16)

    for pred, make in pending:

        @pl.when(pred)
        def _(make=make):
            make().wait_send()


def per_device(leaf, middle, root, s2, s1, o2, o1):
    vmem = pl.BlockSpec(memory_space=pltpu.VMEM)
    smem = pl.BlockSpec(memory_space=pltpu.SMEM)
    dma = pltpu.SemaphoreType.DMA
    outs = [
        jax.ShapeDtypeStruct((8, 1, 8, W), BF16),
        jax.ShapeDtypeStruct((4, 1, 8, W), BF16),
        jax.ShapeDtypeStruct((2, 1, 8, W), BF16),
        jax.ShapeDtypeStruct((2, W, 1, W), BF16),
    ]
    tile = (W, W)
    scratch = [
        pltpu.VMEM((4, 2) + tile, F32),
        pltpu.VMEM((2, 2) + tile, F32),
        pltpu.VMEM(tile, F32),
        pltpu.VMEM((8,) + tile, BF16),
        pltpu.VMEM((8, 2, 2) + tile, BF16),
        pltpu.VMEM(tile, F32),
        pltpu.VMEM((2,) + tile, BF16),
        pltpu.VMEM(tile, F32),
        pltpu.VMEM(tile, F32),
        pltpu.VMEM(tile, F32),
        pltpu.VMEM((4, 3) + tile, BF16),
        pltpu.VMEM((2, 3) + tile, BF16),
        pltpu.VMEM((2,) + tile, F32),
        pltpu.VMEM((2,) + tile, F32),
        pltpu.VMEM((4, 2, 8, W), F32),
        pltpu.VMEM((4, 2, 8, W), F32),
        pltpu.VMEM((2, 2, 8, W), F32),
        pltpu.VMEM((2, 2, 8, W), F32),
        dma((SENDS,)),
        dma((4, 2)), dma((2, 2)), dma, dma((8,)), dma((8, 2, 2)),
        dma((3,)), dma, dma((3,)), dma((3,)), dma((4,)), dma((2,)),
    ]
    return pl.pallas_call(
        kernel,
        out_shape=outs,
        in_specs=[vmem] * 5 + [smem] * 2,
        out_specs=[vmem] * 4,
        scratch_shapes=scratch,
        compiler_params=pltpu.CompilerParams(has_side_effects=True, vmem_limit_bytes=60 * 2**20),
        name="window",
    )(leaf.reshape(8, W, W), middle.reshape(4, W, W), root.reshape(2, W, W), s2, s1, o2, o1)


SENDS = 420


def solution(mesh):
    return jax.shard_map(
        per_device,
        mesh=mesh,
        in_specs=(P(None, "cube", None, "tile"),) * 3 + (P(),) * 4,
        out_specs=(P(None, "cube", "tile", None),) * 3 + (P(None, "cube", None, "tile"),),
        check_vma=False,
    )
```

```python
import jax
import jax.numpy as jnp
from jax import lax
from jax.experimental import pallas as pl
from jax.experimental.pallas import tpu as pltpu
from jax.sharding import PartitionSpec as P

MESH = pl.DeviceIdType.MESH
HIGHEST = lax.Precision.HIGHEST
F32, BF16 = jnp.float32, jnp.bfloat16
W = 256
TREES = (
    ((0, 3), (0, 1), (3, 5), (3, 4), (1, 2), (5, 7), (5, 6)),
    ((1, 4), (1, 2), (1, 0), (4, 6), (4, 5), (2, 3), (6, 7)),
    ((2, 5), (2, 3), (2, 1), (5, 7), (5, 6), (3, 4), (1, 0)),
)


def dot(a, b, ca, cb, precision=None):
    return lax.dot_general(
        a, b, (((ca,), (cb,)), ((), ())), precision=precision, preferred_element_type=F32
    )


def inverse_factor_128(a):
    n = a.shape[0]
    rows = lax.broadcasted_iota(jnp.int32, (n, 1), 0)
    first = lax.broadcasted_iota(jnp.int32, (8, 1), 0)
    eye = lax.broadcasted_iota(jnp.int32, (n, n), 0) == lax.broadcasted_iota(jnp.int32, (n, n), 1)

    def trip(block, ab):
        a, b = ab
        live = rows < n - 8 * block
        pivots = jnp.ones((8, 1), F32)
        for i in range(8):
            row_a, row_b = a[i : i + 1, :], b[i : i + 1, :]
            pivot = a[i : i + 1, i : i + 1]
            pivots = jnp.where(first == i, pivot, pivots)
            scale = jnp.where(live & (rows > i), a[:, i : i + 1] * (1.0 / pivot), 0.0)
            a = a - scale * row_a
            b = b - scale * row_b
        b = jnp.concatenate([b[8:], b[:8] * lax.rsqrt(pivots)], 0)
        a = pltpu.roll(jnp.concatenate([a[8:], a[:8]], 0), n - 8, 1)
        return a, b

    return lax.fori_loop(0, n // 8, trip, (a, eye.astype(F32)))[1]


def inverse_factor(source, target):
    h = W // 2
    i11 = inverse_factor_128(source[:h, :h])
    l21 = dot(source[h:, :h], i11, 1, 1, HIGHEST)
    i22 = inverse_factor_128(source[h:, h:] - dot(l21, l21, 1, 1, HIGHEST))
    i21 = -dot(i22, dot(l21, i11, 1, 0, HIGHEST), 1, 0, HIGHEST)
    target[:h, :h] = i11
    target[:h, h:] = jnp.zeros((h, h), F32)
    target[h:, :h] = i21
    target[h:, h:] = i22


def solve_panel(row_block, inverse):
    return dot(row_block, inverse, 0, 1, HIGHEST)


def place(left, block, right):
    high = block.astype(BF16)
    low = (block - high.astype(F32)).astype(BF16)
    total = None
    for part in (high, low):
        moved = dot(left, part, 1, 0).astype(BF16)
        moved = dot(moved, right, 1, 1)
        total = moved if total is None else total + moved
    return total


def kernel(
    a2, a1, a0, s2, s1, o2, o1,
    leaf_out, mid_out, root_out, schur_out,
    ta2, ta1, pa, cb, rb, li, yb, l1i, l0i, hs, pl2, pm1, acc, ts, psend, precv, msend, mrecv, rel, vb, hp,
    send_sem, r_ta2, r_ta1, r_pa, r_cb, r_rb, r_li, r_yb, r_l1, r_l0, r_ps, r_ms, r_rel, r_vb,
):
    cube, t = lax.axis_index("cube"), lax.axis_index("tile")
    x, zh, c = cube // 4, (cube // 2) % 2, cube % 2
    y, zl = t // 8, t % 8
    g = 2 * zh + c
    mover = c == zh
    pending = []

    def dev(x_, zh_, c_, y_, zl_):
        return (x_ * 4 + zh_ * 2 + c_, y_ * 8 + zl_)

    def send(pred, src, dst, recv, target):
        index = len(pending)

        def make():
            return pltpu.make_async_remote_copy(
                src_ref=src, dst_ref=dst, send_sem=send_sem.at[index], recv_sem=recv,
                device_id=target(), device_id_type=MESH,
            )

        assert index < SENDS
        pending.append((pred, make))

        @pl.when(pred)
        def _():
            make().start()

    def arrive(pred, dst, recv):
        @pl.when(pred)
        def _():
            pltpu.make_async_remote_copy(
                src_ref=dst, dst_ref=dst, send_sem=send_sem.at[0], recv_sem=recv,
                device_id=(cube, t), device_id_type=MESH,
            ).wait_recv()

    always = x >= 0
    is_pd0 = (zh == 0) & (c == 0)
    is_pd1 = (zh == 0) & (c == 1) & (x % 2 == 0)
    is_pd2 = (x == 0) & (zh == 1) & (c == 0)

    send((zh == 0) & (c == 1) & (x % 2 == 1), a2.at[0], pa, r_pa, lambda: dev(x - 1, zh, c, y, zl))
    xo = (x + 2) % 4

    def exchange(who):
        for step in (1, 3):
            xd = (x + step) % 4
            r = step // 2
            for j, src in ((0, a2.at[4 * r + xo]), (1, a1.at[2 * r + xo // 2])):
                send(who, src, rel.at[r, j], r_rel.at[r, j], lambda xd=xd: dev(xd, zh, c, y, zl))
        for step in (1, 3):
            xd = (x + step) % 4
            for r in range(2):
                send(who, a2.at[4 * r + xd], ta2.at[x, r], r_ta2.at[x, r], lambda xd=xd: dev(xd, zh, c, y, zl))

    def pass_on(who):
        for step in (1, 3):
            xd, xs = (x + step) % 4, (x + 4 - step) % 4
            r = step // 2
            for j, dst, recv in ((0, ta2.at[xs, r], r_ta2.at[xs, r]), (1, ta1.at[xs // 2, r], r_ta1.at[xs // 2, r])):
                arrive(who, rel.at[r, j], r_rel.at[r, j])
                send(who, rel.at[r, j], dst, recv, lambda xd=xd: dev(xd, zh, c, y, zl))

    late = t == 1
    exchange(jnp.logical_not(late))
    for r in range(2):
        ta2[x, r] = a2[4 * r + x]
        ta1[x // 2, r] = a1[2 * r + x // 2]

    slot = lax.broadcasted_iota(jnp.int32, (W, W), 0)
    offset = lax.broadcasted_iota(jnp.int32, (1, W), 1)

    def mover_matrix(table, orders, front, tile, pivot):
        keep = (tile * W + offset < orders[front]) & (tile != pivot)
        hit = (table[front, pl.ds(tile, 1), :] == slot) & keep
        return jnp.where(hit, 1.0, 0.0).astype(BF16)

    row_tiles = (4 * x + g, 4 * x + g + 16)

    @pl.loop(0, 4)
    def _(l):
        for w, tile in enumerate(row_tiles + (t,)):
            pl2[l, w] = mover_matrix(s2, o2, l, tile, 0)

    @pl.loop(0, 2)
    def _(m):
        for w, tile in enumerate(row_tiles + (t,)):
            pm1[m, w] = mover_matrix(s1, o1, m, tile, 1)

    lower = lax.broadcasted_iota(jnp.int32, (W, W), 0) >= lax.broadcasted_iota(jnp.int32, (W, W), 1)

    half = W // 2

    def pieces(ref, recv):
        return (
            (ref.at[:half, :half], recv.at[0]),
            (ref.at[half : half + half // 2], recv.at[1]),
            (ref.at[half + half // 2 :], recv.at[2]),
        )

    def clear_upper(ref):
        ref[:half, half:] = jnp.zeros((half, half), F32)

    def fan_out(who, ref, recv, root_zl, ch):
        arrive(who & ((y != 0) | (zl != root_zl)), ref, recv)
        for at, other in TREES[root_zl]:
            send(who & (y == 0) & (zl == at), ref, ref, recv, lambda o=other: dev(x, 0, ch, 0, o))
        for other in (1, 3, 2):
            send(who & (y == 0), ref, ref, recv, lambda o=other: dev(x, 0, ch, o, zl))

    busy = is_pd0 & (t == 0)
    pass_on(jnp.logical_not(late | busy))

    @pl.when(is_pd0 & (t == 0))
    def _():
        inverse_factor(a2.at[0], li)

    @pl.when(jnp.logical_not(is_pd0 & (t == 0)))
    def _():
        clear_upper(li)

    for part, recv in pieces(li, r_li):
        fan_out(is_pd0, part, recv, 0, 0)

    pass_on(busy)

    @pl.when(is_pd0)
    def _():
        panel = solve_panel(a2[0], li[...])
        cb[x] = jnp.where(lower | (t != 0), panel, 0.0).astype(BF16)

    def column_stage(k, holder, own, known):
        arrive(mover & jnp.logical_not(own), cb.at[k], r_cb.at[k])
        send(mover & jnp.logical_not(known), cb.at[k], cb.at[k], r_cb.at[k], lambda: dev(x, zh, 1 - c, y, zl))
        for apart in (1, 3, 2):
            send(mover & holder, cb.at[k], cb.at[k], r_cb.at[k], lambda a=apart: dev((x + a) % 4, zh, c, y, zl))

    def line(r):
        return mover & (y == x // 2 + 2 * r)

    def row_stage(k):
        z0 = 4 * (x % 2) + 2 * zh
        for cc in range(2):
            for r in range(2):
                at = z0 + cc
                source = line(r) & (zl == at)
                ref, recv = rb.at[k, r, cc], r_rb.at[k, r, cc]

                @pl.when(source)
                def _():
                    rb[k, r, cc] = cb[k]

                arrive(line(r) & (zl != at), ref, recv)
                send(line(r) & (zl >= at) & (zl < 7), ref, ref, recv, lambda: dev(x, zh, c, y, zl + 1))
                send(line(r) & (zl <= at) & (zl > 0), ref, ref, recv, lambda: dev(x, zh, c, y, zl - 1))
                for apart in (1, 3, 2):
                    send(line(r), ref, ref, recv, lambda a=apart, cc=cc: dev(x, zh, cc, (y + a) % 4, zl))
                send(line(r) & (c != cc), ref, ref, recv, lambda: dev(x, zh, 1 - c, y, zl))

    def rows_here(k):
        for r in range(2):
            arrive(jnp.logical_not(line(r)), rb.at[k, r, c], r_rb.at[k, r, c])

    for l in range(4):
        send(is_pd0 & (x == l), cb.at[l], cb.at[l], r_cb.at[l], lambda: dev(x, 1, 1, y, zl))
    for l in range(4):
        column_stage(l, x == l, is_pd0 & (x == l), always & False)
    def root_tiles(who):
        for l in range(4):
            for r in range(2):
                arrive(who & (x != l), ta2.at[l, r], r_ta2.at[l, r])
        for m in range(2):
            for r in range(2):
                arrive(who & (x // 2 != m), ta1.at[m, r], r_ta1.at[m, r])

        @pl.when(who)
        def _():
            @pl.loop(0, 2)
            def _(r):
                ts[0] = ta1[0, r]
                ts[1] = ta1[1, r]

                @pl.loop(0, 4)
                def _(l):
                    ts[l // 2] += place(pl2[l, r], ta2[l, r], pl2[l, 2])

                acc[r] = a0[r]

                @pl.loop(0, 2)
                def _(m):
                    acc[r] += place(pm1[m, r], ts[m], pm1[m, 2])

    exchange(late)
    pass_on(late & jnp.logical_not(mover))
    early = (zh == 1) & (c == 0)
    root_tiles(early)

    @pl.when(is_pd2)
    def _():
        high = acc[0].astype(BF16)
        cb[6] = high
        cb[7] = (acc[0] - high.astype(F32)).astype(BF16)

    for k in (6, 7):
        send(is_pd2, cb.at[k], cb.at[k], r_cb.at[k], lambda: dev(0, 1, 1, y, zl))
        send(is_pd2, cb.at[k], cb.at[k], r_cb.at[k], lambda: dev(0, 0, 0, y, zl))

    def carried(m, w, block):
        return dot(pm1[m, w], block, 1, 0).astype(BF16)

    def column_of(k):
        if k < 4:
            return carried(k // 2, 2, dot(pl2[k, 2], cb[k], 1, 0).astype(BF16))
        return carried(k - 4, 2, cb[k])

    def pivot_stage(k):
        @pl.when(mover & (t == 2))
        def _():
            vb[k] = column_of(k)

        zero = mover & (y == 0)
        arrive(zero & (zl != 2), vb.at[k], r_vb.at[k])
        send(zero & (zl >= 2) & (zl < 7), vb.at[k], vb.at[k], r_vb.at[k], lambda: dev(x, zh, c, y, zl + 1))
        send(zero & (zl <= 2) & (zl > 0), vb.at[k], vb.at[k], r_vb.at[k], lambda: dev(x, zh, c, y, zl - 1))
        for other in (1, 3, 2):
            send(zero, vb.at[k], vb.at[k], r_vb.at[k], lambda o=other: dev(x, zh, c, o, zl))
        send(zero, vb.at[k], vb.at[k], r_vb.at[k], lambda: dev(x, zh, 1 - c, y, zl))

    for l in range(4):
        arrive(jnp.logical_not(mover), cb.at[l], r_cb.at[l])

    arrive(is_pd1, pa, r_pa)

    @pl.when(is_pd1)
    def _():
        total = a1[0]
        for i in range(2):
            block = a2[0] if i == 0 else pa[...]
            left = mover_matrix(s2, o2, x + i, 1, 0)
            total = total + place(left, block, pl2[x + i, 2])
        hs[...] = total

        @pl.when(t == 1)
        def _():
            for i in range(2):
                yb[i] = dot(pl2[x + i, 2], cb[x + i], 1, 0).astype(BF16)

    for i in range(2):
        fan_out(is_pd1, yb.at[i], r_yb.at[i], 1, 1)

    @pl.when(is_pd1)
    def _():
        total = hs[...]
        for i in range(2):
            mine = dot(pl2[x + i, 2], cb[x + i], 1, 0).astype(BF16)
            total = total - dot(yb[i], mine, 1, 1)
        hs[...] = total

        @pl.when(t == 1)
        def _():
            inverse_factor(hs, l1i)

    @pl.when(jnp.logical_not(is_pd1 & (t == 1)))
    def _():
        clear_upper(l1i)

    for part, recv in pieces(l1i, r_l1):
        fan_out(is_pd1, part, recv, 1, 1)

    @pl.when(is_pd1)
    def _():
        panel = solve_panel(hs[...], l1i[...])
        cb[4 + x // 2] = jnp.where(lower | (t != 1), panel, 0.0).astype(BF16)

    for m in range(2):
        mine = is_pd1 & (x == 2 * m)
        send(mine, cb.at[4 + m], cb.at[4 + m], r_cb.at[4 + m], lambda: dev(x, 0, 0, y, zl))
        send(mine, cb.at[4 + m], cb.at[4 + m], r_cb.at[4 + m], lambda: dev(x, 1, 1, y, zl))

    for l in range(4):
        row_stage(l)
    for l in range(4):
        pivot_stage(l)
    pass_on(late & mover)
    root_tiles(jnp.logical_not(early))
    for k in (6, 7):
        column_stage(k, x == 0, always & False, (zh == 1) & (x == 0))
    for k in (6, 7):
        row_stage(k)
    for m in range(2):
        column_stage(4 + m, x == 2 * m, always & False, (zh == 0) & (x == 2 * m))
    for m in range(2):
        arrive(jnp.logical_not(mover) & jnp.logical_not(is_pd1 & (x == 2 * m)), cb.at[4 + m], r_cb.at[4 + m])

    root = is_pd2 & (t == 2)

    @pl.when(root)
    def _():
        total = acc[0]
        for k in range(6):
            block = column_of(k)
            total = total - dot(block, block, 1, 1)
        hs[...] = total
        inverse_factor(hs, l0i)

    @pl.when(jnp.logical_not(root))
    def _():
        clear_upper(l0i)

    for part, recv in pieces(l0i, r_l0):
        send(root, part, part, recv, lambda: dev(0, 1, 1, 0, 2))

    for m in range(2):
        row_stage(4 + m)
    for m in range(2):
        pivot_stage(4 + m)
    for k in range(6):
        arrive(mover & (y != 0), vb.at[k], r_vb.at[k])
        send(mover & (y != 0), vb.at[k], vb.at[k], r_vb.at[k], lambda: dev(x, zh, 1 - c, y, zl))
    for l in range(4):
        rows_here(l)
    for k in range(4):
        arrive(jnp.logical_not(mover), vb.at[k], r_vb.at[k])

    pick = (
        lax.broadcasted_iota(jnp.int32, (8, W), 0) + 8 * t == lax.broadcasted_iota(jnp.int32, (8, W), 1)
    )
    pick = jnp.where(pick, 1.0, 0.0).astype(BF16)

    hp[...] = jnp.zeros_like(hp)

    @pl.loop(0, 4)
    def _(l):
        m = l // 2
        col = carried(m, 2, dot(pl2[l, 2], cb[l], 1, 0).astype(BF16))
        for r in range(2):
            psend[l, r] = dot(pick, rb[l, r, c], 1, 0)
            row = carried(m, r, dot(pl2[l, r], rb[l, r, c], 1, 0).astype(BF16))
            acc[r] -= dot(row, col, 1, 1)
            hp[r] -= dot(vb[l], row, 1, 1)
        hp[2] -= dot(vb[l], col, 1, 1)

    for apart in (1, 3, 2):
        xd = (x + apart) % 4
        send(always, psend.at[xd], precv.at[x], r_ps.at[x], lambda xd=xd: dev(xd, zh, c, y, zl))
    precv[x] = psend[x]

    two = mover & (y == 0) & (zl == 2)
    for part, recv in pieces(l0i, r_l0):
        arrive(jnp.logical_not(root), part, recv)
        send(two & (x == 0) & (zh == 1), part, part, recv, lambda: dev(0, 0, 0, 0, 2))
        for other in (1, 3, 2):
            send(two & (x == 0), part, part, recv, lambda o=other: dev(o, zh, c, 0, 2))
        for other in (1, 3, 2):
            send(two, part, part, recv, lambda o=other: dev(x, zh, c, o, 2))
        for at, other in TREES[2]:
            send(mover & (zl == at), part, part, recv, lambda o=other: dev(x, zh, c, y, o))
        send(
            mover & jnp.logical_not((x == 0) & (zh == 1) & (t == 2)),
            part, part, recv, lambda: dev(x, zh, 1 - c, y, zl),
        )

    for m in range(2):
        rows_here(4 + m)
        arrive(jnp.logical_not(mover), vb.at[4 + m], r_vb.at[4 + m])

    @pl.loop(0, 2)
    def _(m):
        col = carried(m, 2, cb[4 + m])
        for r in range(2):
            msend[m, r] = dot(pick, rb[4 + m, r, c], 1, 0)
            row = carried(m, r, rb[4 + m, r, c])
            acc[r] -= dot(row, col, 1, 1)
            hp[r] -= dot(vb[4 + m], row, 1, 1)
        hp[2] -= dot(vb[4 + m], col, 1, 1)

    send(always, msend.at[xo // 2], mrecv.at[x // 2], r_ms.at[x // 2], lambda: dev(xo, zh, c, y, zl))
    mrecv[x // 2] = msend[x // 2]

    for k in (6, 7):
        arrive(jnp.logical_not(mover) & jnp.logical_not(is_pd2), cb.at[k], r_cb.at[k])
        rows_here(k)

    def last_panel(w, high, low):
        return solve_panel(hp[w] + high.astype(F32) + low.astype(F32), l0i[...])

    col = last_panel(2, cb[6], cb[7])
    col = jnp.where(t == 2, 0.0, col).astype(BF16)
    for r in range(2):
        tile = row_tiles[r]
        full = last_panel(r, rb[6, r, c], rb[7, r, c])
        full = jnp.where(lower | (tile != 2), full, 0.0).astype(BF16)
        root_out[r, 0] = dot(pick, full, 1, 0).astype(BF16)
        row = jnp.where(tile == 2, jnp.zeros_like(full), full)
        schur_out[r, :, 0, :] = (acc[r] - dot(row, col, 1, 1)).astype(BF16)

    for s in range(4):
        arrive(x != s, precv.at[s], r_ps.at[s])
    for s in range(2):
        arrive(x // 2 != s, mrecv.at[s], r_ms.at[s])
    for s in range(4):
        for r in range(2):
            leaf_out[4 * r + s, 0] = precv[s, r].astype(BF16)
    for s in range(2):
        for r in range(2):
            mid_out[2 * r + s, 0] = mrecv[s, r].astype(BF16)

    for pred, make in pending:

        @pl.when(pred)
        def _(make=make):
            make().wait_send()


def per_device(leaf, middle, root, s2, s1, o2, o1):
    vmem = pl.BlockSpec(memory_space=pltpu.VMEM)
    smem = pl.BlockSpec(memory_space=pltpu.SMEM)
    dma = pltpu.SemaphoreType.DMA
    outs = [
        jax.ShapeDtypeStruct((8, 1, 8, W), BF16),
        jax.ShapeDtypeStruct((4, 1, 8, W), BF16),
        jax.ShapeDtypeStruct((2, 1, 8, W), BF16),
        jax.ShapeDtypeStruct((2, W, 1, W), BF16),
    ]
    tile = (W, W)
    scratch = [
        pltpu.VMEM((4, 2) + tile, F32),
        pltpu.VMEM((2, 2) + tile, F32),
        pltpu.VMEM(tile, F32),
        pltpu.VMEM((8,) + tile, BF16),
        pltpu.VMEM((8, 2, 2) + tile, BF16),
        pltpu.VMEM(tile, F32),
        pltpu.VMEM((2,) + tile, BF16),
        pltpu.VMEM(tile, F32),
        pltpu.VMEM(tile, F32),
        pltpu.VMEM(tile, F32),
        pltpu.VMEM((4, 3) + tile, BF16),
        pltpu.VMEM((2, 3) + tile, BF16),
        pltpu.VMEM((2,) + tile, F32),
        pltpu.VMEM((2,) + tile, F32),
        pltpu.VMEM((4, 2, 8, W), F32),
        pltpu.VMEM((4, 2, 8, W), F32),
        pltpu.VMEM((2, 2, 8, W), F32),
        pltpu.VMEM((2, 2, 8, W), F32),
        pltpu.VMEM((2, 2) + tile, F32),
        pltpu.VMEM((6,) + tile, BF16),
        pltpu.VMEM((3,) + tile, F32),
        dma((SENDS,)),
        dma((4, 2)), dma((2, 2)), dma, dma((8,)), dma((8, 2, 2)),
        dma((3,)), dma((2,)), dma((3,)), dma((3,)), dma((4,)), dma((2,)), dma((2, 2)), dma((6,)),
    ]
    return pl.pallas_call(
        kernel,
        out_shape=outs,
        in_specs=[vmem] * 5 + [smem] * 2,
        out_specs=[vmem] * 4,
        scratch_shapes=scratch,
        compiler_params=pltpu.CompilerParams(has_side_effects=True, vmem_limit_bytes=60 * 2**20),
        name="window",
    )(leaf.reshape(8, W, W), middle.reshape(4, W, W), root.reshape(2, W, W), s2, s1, o2, o1)


SENDS = 480


def solution(mesh):
    return jax.shard_map(
        per_device,
        mesh=mesh,
        in_specs=(P(None, "cube", None, "tile"),) * 3 + (P(),) * 4,
        out_specs=(P(None, "cube", "tile", None),) * 3 + (P(None, "cube", None, "tile"),),
        check_vma=False,
    )
```

```python
import jax
import jax.numpy as jnp
from jax import lax
from jax.experimental import pallas as pl
from jax.experimental.pallas import tpu as pltpu
from jax.sharding import PartitionSpec as P

MESH = pl.DeviceIdType.MESH
HIGHEST = lax.Precision.HIGHEST
F32, BF16 = jnp.float32, jnp.bfloat16
W = 256
TREES = (
    ((0, 3), (0, 1), (3, 5), (3, 4), (1, 2), (5, 7), (5, 6)),
    ((1, 4), (1, 2), (1, 0), (4, 6), (4, 5), (2, 3), (6, 7)),
    ((2, 5), (2, 3), (2, 1), (5, 7), (5, 6), (3, 4), (1, 0)),
)


def dot(a, b, ca, cb, precision=None):
    return lax.dot_general(
        a, b, (((ca,), (cb,)), ((), ())), precision=precision, preferred_element_type=F32
    )


def inverse_factor_128(a):
    n = a.shape[0]
    rows = lax.broadcasted_iota(jnp.int32, (n, 1), 0)
    first = lax.broadcasted_iota(jnp.int32, (8, 1), 0)
    eye = lax.broadcasted_iota(jnp.int32, (n, n), 0) == lax.broadcasted_iota(jnp.int32, (n, n), 1)

    def trip(block, ab):
        a, b = ab
        live = rows < n - 8 * block
        pivots = jnp.ones((8, 1), F32)
        for i in range(8):
            row_a, row_b = a[i : i + 1, :], b[i : i + 1, :]
            pivot = a[i : i + 1, i : i + 1]
            pivots = jnp.where(first == i, pivot, pivots)
            scale = jnp.where(live & (rows > i), a[:, i : i + 1] * (1.0 / pivot), 0.0)
            a = a - scale * row_a
            b = b - scale * row_b
        b = jnp.concatenate([b[8:], b[:8] * lax.rsqrt(pivots)], 0)
        a = pltpu.roll(jnp.concatenate([a[8:], a[:8]], 0), n - 8, 1)
        return a, b

    return lax.fori_loop(0, n // 8, trip, (a, eye.astype(F32)))[1]


def inverse_factor(source, target):
    h = W // 2
    i11 = inverse_factor_128(source[:h, :h])
    l21 = dot(source[h:, :h], i11, 1, 1, HIGHEST)
    i22 = inverse_factor_128(source[h:, h:] - dot(l21, l21, 1, 1, HIGHEST))
    i21 = -dot(i22, dot(l21, i11, 1, 0, HIGHEST), 1, 0, HIGHEST)
    target[:h, :h] = i11
    target[:h, h:] = jnp.zeros((h, h), F32)
    target[h:, :h] = i21
    target[h:, h:] = i22


def solve_panel(row_block, inverse):
    return dot(row_block, inverse, 0, 1, HIGHEST)


def place(left, block, right):
    high = block.astype(BF16)
    low = (block - high.astype(F32)).astype(BF16)
    total = None
    for part in (high, low):
        moved = dot(left, part, 1, 0).astype(BF16)
        moved = dot(moved, right, 1, 1)
        total = moved if total is None else total + moved
    return total


def kernel(
    a2, a1, a0, s2, s1, o2, o1,
    leaf_out, mid_out, root_out, schur_out,
    ta2, ta1, pa, cb, rb, li, yb, l1i, l0i, hs, pl2, pm1, acc, ts, psend, precv, msend, mrecv, rel, vb, hp,
    send_sem, r_ta2, r_ta1, r_pa, r_cb, r_rb, r_li, r_yb, r_l1, r_l0, r_ps, r_ms, r_rel, r_vb,
):
    cube, t = lax.axis_index("cube"), lax.axis_index("tile")
    x, zh, c = cube // 4, (cube // 2) % 2, cube % 2
    y, zl = t // 8, t % 8
    g = 2 * zh + c
    mover = c == zh
    pending = []

    def dev(x_, zh_, c_, y_, zl_):
        return (x_ * 4 + zh_ * 2 + c_, y_ * 8 + zl_)

    def send(pred, src, dst, recv, target):
        index = len(pending)

        def make():
            return pltpu.make_async_remote_copy(
                src_ref=src, dst_ref=dst, send_sem=send_sem.at[index], recv_sem=recv,
                device_id=target(), device_id_type=MESH,
            )

        assert index < SENDS
        pending.append((pred, make))

        @pl.when(pred)
        def _():
            make().start()

    def arrive(pred, dst, recv):
        @pl.when(pred)
        def _():
            pltpu.make_async_remote_copy(
                src_ref=dst, dst_ref=dst, send_sem=send_sem.at[0], recv_sem=recv,
                device_id=(cube, t), device_id_type=MESH,
            ).wait_recv()

    always = x >= 0
    is_pd0 = (zh == 0) & (c == 0)
    is_pd1 = (zh == 0) & (c == 1) & (x % 2 == 0)
    is_pd2 = (x == 0) & (zh == 1) & (c == 0)

    xo = (x + 2) % 4

    def exchange(who):
        for step in (1, 3):
            xd = (x + step) % 4
            r = step // 2
            for j, src in ((0, a2.at[4 * r + xo]), (1, a1.at[2 * r + xo // 2])):
                send(who, src, rel.at[r, j], r_rel.at[r, j], lambda xd=xd: dev(xd, zh, c, y, zl))
        for step in (1, 3):
            xd = (x + step) % 4
            for r in range(2):
                send(who, a2.at[4 * r + xd], ta2.at[x, r], r_ta2.at[x, r], lambda xd=xd: dev(xd, zh, c, y, zl))

    def pass_on(who):
        for step in (1, 3):
            xd, xs = (x + step) % 4, (x + 4 - step) % 4
            r = step // 2
            for j, dst, recv in ((0, ta2.at[xs, r], r_ta2.at[xs, r]), (1, ta1.at[xs // 2, r], r_ta1.at[xs // 2, r])):
                arrive(who, rel.at[r, j], r_rel.at[r, j])
                send(who, rel.at[r, j], dst, recv, lambda xd=xd: dev(xd, zh, c, y, zl))

    late = t == 1
    busy = is_pd0 & (t == 0)

    barrier = pltpu.get_barrier_semaphore()

    def signal(target):
        pl.semaphore_signal(barrier, inc=1, device_id=target, device_id_type=MESH)

    for apart in (1, 2, 3):
        signal(dev((x + apart) % 4, zh, c, y, zl))
        for cc in range(2):
            signal(dev(x, zh, cc, (y + apart) % 4, zl))
    signal(dev(x, zh, 1 - c, y, zl))
    for cc in range(2):
        signal(dev(x, 1 - zh, cc, y, zl))
    for apart in (-3, -2, -1, 1, 2, 3):

        @pl.when((zl + apart >= 0) & (zl + apart < 8))
        def _(apart=apart):
            signal(dev(x, zh, c, y, zl + apart))

    for r in range(2):
        ta2[x, r] = a2[4 * r + x]
        ta1[x // 2, r] = a1[2 * r + x // 2]

    slot = lax.broadcasted_iota(jnp.int32, (W, W), 0)
    offset = lax.broadcasted_iota(jnp.int32, (1, W), 1)

    def mover_matrix(table, orders, front, tile, pivot):
        keep = (tile * W + offset < orders[front]) & (tile != pivot)
        hit = (table[front, pl.ds(tile, 1), :] == slot) & keep
        return jnp.where(hit, 1.0, 0.0).astype(BF16)

    row_tiles = (4 * x + g, 4 * x + g + 16)

    @pl.loop(0, 4)
    def _(l):
        for w, tile in enumerate(row_tiles + (t,)):
            pl2[l, w] = mover_matrix(s2, o2, l, tile, 0)

    @pl.loop(0, 2)
    def _(m):
        for w, tile in enumerate(row_tiles + (t,)):
            pm1[m, w] = mover_matrix(s1, o1, m, tile, 1)

    lower = lax.broadcasted_iota(jnp.int32, (W, W), 0) >= lax.broadcasted_iota(jnp.int32, (W, W), 1)

    half = W // 2

    def pieces(ref, recv):
        return (
            (ref.at[:half, :half], recv.at[0]),
            (ref.at[half : half + half // 2], recv.at[1]),
            (ref.at[half + half // 2 :], recv.at[2]),
        )

    def clear_upper(ref):
        ref[:half, half:] = jnp.zeros((half, half), F32)

    def fan_out(who, ref, recv, root_zl, ch):
        arrive(who & ((y != 0) | (zl != root_zl)), ref, recv)
        for at, other in TREES[root_zl]:
            send(who & (y == 0) & (zl == at), ref, ref, recv, lambda o=other: dev(x, 0, ch, 0, o))
        for other in (1, 3, 2):
            send(who & (y == 0), ref, ref, recv, lambda o=other: dev(x, 0, ch, o, zl))

    @pl.when(busy)
    def _():
        inverse_factor(a2.at[0], li)

    pl.semaphore_wait(barrier, 12 + jnp.minimum(zl, 3) + jnp.minimum(7 - zl, 3))

    send((zh == 0) & (c == 1) & (x % 2 == 1), a2.at[0], pa, r_pa, lambda: dev(x - 1, zh, c, y, zl))
    exchange(jnp.logical_not(late | busy))
    pass_on(jnp.logical_not(late | busy))

    @pl.when(jnp.logical_not(is_pd0 & (t == 0)))
    def _():
        clear_upper(li)

    for part, recv in pieces(li, r_li):
        fan_out(is_pd0, part, recv, 0, 0)

    exchange(busy)
    pass_on(busy)

    @pl.when(is_pd0)
    def _():
        panel = solve_panel(a2[0], li[...])
        cb[x] = jnp.where(lower | (t != 0), panel, 0.0).astype(BF16)

    def column_stage(k, holder, own, known):
        arrive(mover & jnp.logical_not(own), cb.at[k], r_cb.at[k])
        send(mover & jnp.logical_not(known), cb.at[k], cb.at[k], r_cb.at[k], lambda: dev(x, zh, 1 - c, y, zl))
        for apart in (1, 3, 2):
            send(mover & holder, cb.at[k], cb.at[k], r_cb.at[k], lambda a=apart: dev((x + a) % 4, zh, c, y, zl))

    def line(r):
        return mover & (y == x // 2 + 2 * r)

    def halves(k, ref, recv):
        if k in (4, 5):
            return ((ref.at[:half], recv.at[0]), (ref.at[half:], recv.at[1]))
        return ((ref, recv.at[0]),)

    def row_stage(k):
        z0 = 4 * (x % 2) + 2 * zh
        for cc in range(2):
            for r in range(2):
                at = z0 + cc
                source = line(r) & (zl == at)
                ref = rb.at[k, r, cc]

                @pl.when(source)
                def _():
                    rb[k, r, cc] = cb[k]

                for part, recv in halves(k, ref, r_rb.at[k, r, cc]):
                    arrive(line(r) & (zl != at), part, recv)
                    send(line(r) & (zl >= at) & (zl < 7), part, part, recv, lambda: dev(x, zh, c, y, zl + 1))
                    send(line(r) & (zl <= at) & (zl > 0), part, part, recv, lambda: dev(x, zh, c, y, zl - 1))
                    for apart in (1, 3, 2):
                        send(line(r), part, part, recv, lambda a=apart, cc=cc: dev(x, zh, cc, (y + a) % 4, zl))
                    send(line(r) & (c != cc), part, part, recv, lambda: dev(x, zh, 1 - c, y, zl))

    def rows_here(k):
        for r in range(2):
            for part, recv in halves(k, rb.at[k, r, c], r_rb.at[k, r, c]):
                arrive(jnp.logical_not(line(r)), part, recv)

    for l in range(4):
        send(is_pd0 & (x == l), cb.at[l], cb.at[l], r_cb.at[l], lambda: dev(x, 1, 1, y, zl))
    for l in range(4):
        column_stage(l, x == l, is_pd0 & (x == l), always & False)
    def root_tiles(who):
        for l in range(4):
            for r in range(2):
                arrive(who & (x != l), ta2.at[l, r], r_ta2.at[l, r])
        for m in range(2):
            for r in range(2):
                arrive(who & (x // 2 != m), ta1.at[m, r], r_ta1.at[m, r])

        @pl.when(who)
        def _():
            @pl.loop(0, 2)
            def _(r):
                ts[0] = ta1[0, r]
                ts[1] = ta1[1, r]

                @pl.loop(0, 4)
                def _(l):
                    ts[l // 2] += place(pl2[l, r], ta2[l, r], pl2[l, 2])

                acc[r] = a0[r]

                @pl.loop(0, 2)
                def _(m):
                    acc[r] += place(pm1[m, r], ts[m], pm1[m, 2])

    exchange(late)
    pass_on(late & jnp.logical_not(mover))
    early = (zh == 1) & (c == 0)
    root_tiles(early)

    @pl.when(is_pd2)
    def _():
        high = acc[0].astype(BF16)
        cb[6] = high
        cb[7] = (acc[0] - high.astype(F32)).astype(BF16)

    for k in (6, 7):
        send(is_pd2, cb.at[k], cb.at[k], r_cb.at[k], lambda: dev(0, 1, 1, y, zl))
        send(is_pd2, cb.at[k], cb.at[k], r_cb.at[k], lambda: dev(0, 0, 0, y, zl))

    def carried(m, w, block):
        return dot(pm1[m, w], block, 1, 0).astype(BF16)

    def column_of(k):
        if k < 4:
            return carried(k // 2, 2, dot(pl2[k, 2], cb[k], 1, 0).astype(BF16))
        return carried(k - 4, 2, cb[k])

    def pivot_stage(k):
        @pl.when(mover & (t == 2))
        def _():
            vb[k] = column_of(k)

        zero = mover & (y == 0)
        arrive(zero & (zl != 2), vb.at[k], r_vb.at[k])
        send(zero & (zl >= 2) & (zl < 7), vb.at[k], vb.at[k], r_vb.at[k], lambda: dev(x, zh, c, y, zl + 1))
        send(zero & (zl <= 2) & (zl > 0), vb.at[k], vb.at[k], r_vb.at[k], lambda: dev(x, zh, c, y, zl - 1))
        for other in (1, 3, 2):
            send(zero, vb.at[k], vb.at[k], r_vb.at[k], lambda o=other: dev(x, zh, c, o, zl))
        send(zero, vb.at[k], vb.at[k], r_vb.at[k], lambda: dev(x, zh, 1 - c, y, zl))

    for l in range(4):
        arrive(jnp.logical_not(mover), cb.at[l], r_cb.at[l])

    arrive(is_pd1, pa, r_pa)

    @pl.when(is_pd1)
    def _():
        total = a1[0]
        for i in range(2):
            block = a2[0] if i == 0 else pa[...]
            left = mover_matrix(s2, o2, x + i, 1, 0)
            total = total + place(left, block, pl2[x + i, 2])
        hs[...] = total

        @pl.when(t == 1)
        def _():
            for i in range(2):
                yb[i] = dot(pl2[x + i, 2], cb[x + i], 1, 0).astype(BF16)

    for i in range(2):
        fan_out(is_pd1, yb.at[i], r_yb.at[i], 1, 1)

    @pl.when(is_pd1)
    def _():
        total = hs[...]
        for i in range(2):
            mine = dot(pl2[x + i, 2], cb[x + i], 1, 0).astype(BF16)
            total = total - dot(yb[i], mine, 1, 1)
        hs[...] = total

        @pl.when(t == 1)
        def _():
            inverse_factor(hs, l1i)

    @pl.when(jnp.logical_not(is_pd1 & (t == 1)))
    def _():
        clear_upper(l1i)

    for part, recv in pieces(l1i, r_l1):
        fan_out(is_pd1, part, recv, 1, 1)

    @pl.when(is_pd1)
    def _():
        panel = solve_panel(hs[...], l1i[...])
        cb[4 + x // 2] = jnp.where(lower | (t != 1), panel, 0.0).astype(BF16)

    for m in range(2):
        mine = is_pd1 & (x == 2 * m)
        send(mine, cb.at[4 + m], cb.at[4 + m], r_cb.at[4 + m], lambda: dev(x, 0, 0, y, zl))
        send(mine, cb.at[4 + m], cb.at[4 + m], r_cb.at[4 + m], lambda: dev(x, 1, 1, y, zl))

    for l in range(4):
        row_stage(l)
    for l in range(4):
        pivot_stage(l)
    pass_on(late & mover)
    root_tiles(jnp.logical_not(early | late))
    for k in (6, 7):
        column_stage(k, x == 0, always & False, (zh == 1) & (x == 0))
    for k in (6, 7):
        row_stage(k)
    for m in range(2):
        column_stage(4 + m, x == 2 * m, always & False, (zh == 0) & (x == 2 * m))
    for m in range(2):
        arrive(jnp.logical_not(mover) & jnp.logical_not(is_pd1 & (x == 2 * m)), cb.at[4 + m], r_cb.at[4 + m])

    root = is_pd2 & (t == 2)

    @pl.when(root)
    def _():
        total = acc[0]
        for k in range(6):
            block = column_of(k)
            total = total - dot(block, block, 1, 1)
        hs[...] = total
        inverse_factor(hs, l0i)

    @pl.when(jnp.logical_not(root))
    def _():
        clear_upper(l0i)

    for part, recv in pieces(l0i, r_l0):
        send(root, part, part, recv, lambda: dev(0, 1, 1, 0, 2))

    for m in range(2):
        row_stage(4 + m)
    for m in range(2):
        pivot_stage(4 + m)
    root_tiles(late & jnp.logical_not(early))
    for k in range(6):
        arrive(mover & (y != 0), vb.at[k], r_vb.at[k])
        send(mover & (y != 0), vb.at[k], vb.at[k], r_vb.at[k], lambda: dev(x, zh, 1 - c, y, zl))
    for l in range(4):
        rows_here(l)
    for k in range(4):
        arrive(jnp.logical_not(mover), vb.at[k], r_vb.at[k])

    pick = (
        lax.broadcasted_iota(jnp.int32, (8, W), 0) + 8 * t == lax.broadcasted_iota(jnp.int32, (8, W), 1)
    )
    pick = jnp.where(pick, 1.0, 0.0).astype(BF16)

    hp[...] = jnp.zeros_like(hp)

    @pl.loop(0, 4)
    def _(l):
        m = l // 2
        col = carried(m, 2, dot(pl2[l, 2], cb[l], 1, 0).astype(BF16))
        for r in range(2):
            psend[l, r] = dot(pick, rb[l, r, c], 1, 0)
            row = carried(m, r, dot(pl2[l, r], rb[l, r, c], 1, 0).astype(BF16))
            acc[r] -= dot(row, col, 1, 1)
            hp[r] -= dot(vb[l], row, 1, 1)
        hp[2] -= dot(vb[l], col, 1, 1)

    for apart in (1, 3, 2):
        xd = (x + apart) % 4
        send(always, psend.at[xd], precv.at[x], r_ps.at[x], lambda xd=xd: dev(xd, zh, c, y, zl))
    precv[x] = psend[x]

    two = mover & (y == 0) & (zl == 2)
    for part, recv in pieces(l0i, r_l0):
        arrive(jnp.logical_not(root), part, recv)
        send(two & (x == 0) & (zh == 1), part, part, recv, lambda: dev(0, 0, 0, 0, 2))
        for other in (1, 3, 2):
            send(two & (x == 0), part, part, recv, lambda o=other: dev(o, zh, c, 0, 2))
        for other in (1, 3, 2):
            send(two, part, part, recv, lambda o=other: dev(x, zh, c, o, 2))
        for at, other in TREES[2]:
            send(mover & (zl == at), part, part, recv, lambda o=other: dev(x, zh, c, y, o))
        send(
            mover & jnp.logical_not((x == 0) & (zh == 1) & (t == 2)),
            part, part, recv, lambda: dev(x, zh, 1 - c, y, zl),
        )

    for m in range(2):
        rows_here(4 + m)
        arrive(jnp.logical_not(mover), vb.at[4 + m], r_vb.at[4 + m])

    @pl.loop(0, 2)
    def _(m):
        col = carried(m, 2, cb[4 + m])
        for r in range(2):
            msend[m, r] = dot(pick, rb[4 + m, r, c], 1, 0)
            row = carried(m, r, rb[4 + m, r, c])
            acc[r] -= dot(row, col, 1, 1)
            hp[r] -= dot(vb[4 + m], row, 1, 1)
        hp[2] -= dot(vb[4 + m], col, 1, 1)

    send(always, msend.at[xo // 2], mrecv.at[x // 2], r_ms.at[x // 2], lambda: dev(xo, zh, c, y, zl))
    mrecv[x // 2] = msend[x // 2]

    for k in (6, 7):
        arrive(jnp.logical_not(mover) & jnp.logical_not(is_pd2), cb.at[k], r_cb.at[k])
        rows_here(k)

    def last_panel(w, high, low):
        return solve_panel(hp[w] + high.astype(F32) + low.astype(F32), l0i[...])

    col = last_panel(2, cb[6], cb[7])
    col = jnp.where(t == 2, 0.0, col).astype(BF16)
    for r in range(2):
        tile = row_tiles[r]
        full = last_panel(r, rb[6, r, c], rb[7, r, c])
        full = jnp.where(lower | (tile != 2), full, 0.0).astype(BF16)
        root_out[r, 0] = dot(pick, full, 1, 0).astype(BF16)
        row = jnp.where(tile == 2, jnp.zeros_like(full), full)
        schur_out[r] = (acc[r] - dot(row, col, 1, 1)).astype(BF16)

    for s in range(4):
        arrive(x != s, precv.at[s], r_ps.at[s])
    for s in range(2):
        arrive(x // 2 != s, mrecv.at[s], r_ms.at[s])
    for s in range(4):
        for r in range(2):
            leaf_out[4 * r + s, 0] = precv[s, r].astype(BF16)
    for s in range(2):
        for r in range(2):
            mid_out[2 * r + s, 0] = mrecv[s, r].astype(BF16)

    for pred, make in pending:

        @pl.when(pred)
        def _(make=make):
            make().wait_send()


def per_device(leaf, middle, root, s2, s1, o2, o1):
    vmem = pl.BlockSpec(memory_space=pltpu.VMEM)
    smem = pl.BlockSpec(memory_space=pltpu.SMEM)
    dma = pltpu.SemaphoreType.DMA
    outs = [
        jax.ShapeDtypeStruct((8, 1, 8, W), BF16),
        jax.ShapeDtypeStruct((4, 1, 8, W), BF16),
        jax.ShapeDtypeStruct((2, 1, 8, W), BF16),
        jax.ShapeDtypeStruct((2, W, W), BF16),
    ]
    tile = (W, W)
    scratch = [
        pltpu.VMEM((4, 2) + tile, F32),
        pltpu.VMEM((2, 2) + tile, F32),
        pltpu.VMEM(tile, F32),
        pltpu.VMEM((8,) + tile, BF16),
        pltpu.VMEM((8, 2, 2) + tile, BF16),
        pltpu.VMEM(tile, F32),
        pltpu.VMEM((2,) + tile, BF16),
        pltpu.VMEM(tile, F32),
        pltpu.VMEM(tile, F32),
        pltpu.VMEM(tile, F32),
        pltpu.VMEM((4, 3) + tile, BF16),
        pltpu.VMEM((2, 3) + tile, BF16),
        pltpu.VMEM((2,) + tile, F32),
        pltpu.VMEM((2,) + tile, F32),
        pltpu.VMEM((4, 2, 8, W), F32),
        pltpu.VMEM((4, 2, 8, W), F32),
        pltpu.VMEM((2, 2, 8, W), F32),
        pltpu.VMEM((2, 2, 8, W), F32),
        pltpu.VMEM((2, 2) + tile, F32),
        pltpu.VMEM((6,) + tile, BF16),
        pltpu.VMEM((3,) + tile, F32),
        dma((SENDS,)),
        dma((4, 2)), dma((2, 2)), dma, dma((8,)), dma((8, 2, 2, 2)),
        dma((3,)), dma((2,)), dma((3,)), dma((3,)), dma((4,)), dma((2,)), dma((2, 2)), dma((6,)),
    ]
    *panels, schur = pl.pallas_call(
        kernel,
        out_shape=outs,
        in_specs=[vmem] * 5 + [smem] * 2,
        out_specs=[vmem] * 4,
        scratch_shapes=scratch,
        compiler_params=pltpu.CompilerParams(has_side_effects=True, collective_id=0, vmem_limit_bytes=60 * 2**20),
        name="window",
    )(leaf.reshape(8, W, W), middle.reshape(4, W, W), root.reshape(2, W, W), s2, s1, o2, o1)
    return (*panels, schur.reshape(2, W, 1, W))


SENDS = 560


def solution(mesh):
    return jax.shard_map(
        per_device,
        mesh=mesh,
        in_specs=(P(None, "cube", None, "tile"),) * 3 + (P(),) * 4,
        out_specs=(P(None, "cube", "tile", None),) * 3 + (P(None, "cube", None, "tile"),),
        check_vma=False,
    )
```

```python
import jax
import jax.numpy as jnp
from jax import lax
from jax.experimental import pallas as pl
from jax.experimental.pallas import tpu as pltpu
from jax.sharding import PartitionSpec as P

MESH = pl.DeviceIdType.MESH
HIGHEST = lax.Precision.HIGHEST
F32, BF16 = jnp.float32, jnp.bfloat16
W = 256
TREES = (
    ((0, 3), (0, 1), (3, 5), (3, 4), (1, 2), (5, 7), (5, 6)),
    ((1, 4), (1, 2), (1, 0), (4, 6), (4, 5), (2, 3), (6, 7)),
    ((2, 5), (2, 3), (2, 1), (5, 7), (5, 6), (3, 4), (1, 0)),
)


def dot(a, b, ca, cb, precision=None):
    return lax.dot_general(
        a, b, (((ca,), (cb,)), ((), ())), precision=precision, preferred_element_type=F32
    )


def inverse_factor_128(a):
    n = a.shape[0]
    rows = lax.broadcasted_iota(jnp.int32, (n, 1), 0)
    first = lax.broadcasted_iota(jnp.int32, (8, 1), 0)
    eye = lax.broadcasted_iota(jnp.int32, (n, n), 0) == lax.broadcasted_iota(jnp.int32, (n, n), 1)

    def trip(block, ab):
        a, b = ab
        live = rows < n - 8 * block
        pivots = jnp.ones((8, 1), F32)
        for i in range(8):
            row_a, row_b = a[i : i + 1, :], b[i : i + 1, :]
            pivot = a[i : i + 1, i : i + 1]
            pivots = jnp.where(first == i, pivot, pivots)
            scale = jnp.where(live & (rows > i), a[:, i : i + 1] * (1.0 / pivot), 0.0)
            a = a - scale * row_a
            b = b - scale * row_b
        b = jnp.concatenate([b[8:], b[:8] * lax.rsqrt(pivots)], 0)
        a = pltpu.roll(jnp.concatenate([a[8:], a[:8]], 0), n - 8, 1)
        return a, b

    return lax.fori_loop(0, n // 8, trip, (a, eye.astype(F32)))[1]


def inverse_factor(source, target):
    h = W // 2
    i11 = inverse_factor_128(source[:h, :h])
    l21 = dot(source[h:, :h], i11, 1, 1, HIGHEST)
    i22 = inverse_factor_128(source[h:, h:] - dot(l21, l21, 1, 1, HIGHEST))
    i21 = -dot(i22, dot(l21, i11, 1, 0, HIGHEST), 1, 0, HIGHEST)
    target[:h, :h] = i11
    target[:h, h:] = jnp.zeros((h, h), F32)
    target[h:, :h] = i21
    target[h:, h:] = i22


def solve_panel(row_block, inverse):
    return dot(row_block, inverse, 0, 1, HIGHEST)


def place(left, block, right):
    high = block.astype(BF16)
    low = (block - high.astype(F32)).astype(BF16)
    total = None
    for part in (high, low):
        moved = dot(left, part, 1, 0).astype(BF16)
        moved = dot(moved, right, 1, 1)
        total = moved if total is None else total + moved
    return total


def kernel(
    a2, a1, a0, s2, s1, o2, o1,
    leaf_out, mid_out, root_out, schur_out,
    ta2, ta1, pa, cb, rb, li, yb, l1i, l0i, hs, pl2, pm1, acc, ts, psend, precv, msend, mrecv, rel, vb, hp, vx,
    send_sem, r_ta2, r_ta1, r_pa, r_cb, r_rb, r_li, r_yb, r_l1, r_l0, r_ps, r_ms, r_rel, r_vb, r_vx,
):
    cube, t = lax.axis_index("cube"), lax.axis_index("tile")
    x, zh, c = cube // 4, (cube // 2) % 2, cube % 2
    y, zl = t // 8, t % 8
    g = 2 * zh + c
    mover = c == zh
    pending = []

    def dev(x_, zh_, c_, y_, zl_):
        return (x_ * 4 + zh_ * 2 + c_, y_ * 8 + zl_)

    def send(pred, src, dst, recv, target):
        index = len(pending)

        def make():
            return pltpu.make_async_remote_copy(
                src_ref=src, dst_ref=dst, send_sem=send_sem.at[index], recv_sem=recv,
                device_id=target(), device_id_type=MESH,
            )

        assert index < SENDS
        pending.append((pred, make))

        @pl.when(pred)
        def _():
            make().start()

    def arrive(pred, dst, recv):
        @pl.when(pred)
        def _():
            pltpu.make_async_remote_copy(
                src_ref=dst, dst_ref=dst, send_sem=send_sem.at[0], recv_sem=recv,
                device_id=(cube, t), device_id_type=MESH,
            ).wait_recv()

    always = x >= 0
    is_pd0 = (zh == 0) & (c == 0)
    is_pd1 = (zh == 0) & (c == 1) & (x % 2 == 0)
    is_pd2 = (x == 0) & (zh == 1) & (c == 0)

    xo = (x + 2) % 4

    def exchange(who):
        for step in (1, 3):
            xd = (x + step) % 4
            r = step // 2
            for j, src in ((0, a2.at[4 * r + xo]), (1, a1.at[2 * r + xo // 2])):
                send(who, src, rel.at[r, j], r_rel.at[r, j], lambda xd=xd: dev(xd, zh, c, y, zl))
        for step in (1, 3):
            xd = (x + step) % 4
            for r in range(2):
                send(who, a2.at[4 * r + xd], ta2.at[x, r], r_ta2.at[x, r], lambda xd=xd: dev(xd, zh, c, y, zl))

    def pass_on(who):
        for step in (1, 3):
            xd, xs = (x + step) % 4, (x + 4 - step) % 4
            r = step // 2
            for j, dst, recv in ((0, ta2.at[xs, r], r_ta2.at[xs, r]), (1, ta1.at[xs // 2, r], r_ta1.at[xs // 2, r])):
                arrive(who, rel.at[r, j], r_rel.at[r, j])
                send(who, rel.at[r, j], dst, recv, lambda xd=xd: dev(xd, zh, c, y, zl))

    late = t == 1
    busy = is_pd0 & (t == 0)

    barrier = pltpu.get_barrier_semaphore()

    def signal(target):
        pl.semaphore_signal(barrier, inc=1, device_id=target, device_id_type=MESH)

    for apart in (1, 2, 3):
        signal(dev((x + apart) % 4, zh, c, y, zl))
        for cc in range(2):
            signal(dev(x, zh, cc, (y + apart) % 4, zl))
    signal(dev(x, zh, 1 - c, y, zl))
    for cc in range(2):
        signal(dev(x, 1 - zh, cc, y, zl))
    for apart in (-3, -2, -1, 1, 2, 3):

        @pl.when((zl + apart >= 0) & (zl + apart < 8))
        def _(apart=apart):
            signal(dev(x, zh, c, y, zl + apart))

    for r in range(2):
        ta2[x, r] = a2[4 * r + x]
        ta1[x // 2, r] = a1[2 * r + x // 2]

    slot = lax.broadcasted_iota(jnp.int32, (W, W), 0)
    offset = lax.broadcasted_iota(jnp.int32, (1, W), 1)

    def mover_matrix(table, orders, front, tile, pivot):
        keep = (tile * W + offset < orders[front]) & (tile != pivot)
        hit = (table[front, pl.ds(tile, 1), :] == slot) & keep
        return jnp.where(hit, 1.0, 0.0).astype(BF16)

    row_tiles = (4 * x + g, 4 * x + g + 16)

    @pl.loop(0, 4)
    def _(l):
        for w, tile in enumerate(row_tiles + (t,)):
            pl2[l, w] = mover_matrix(s2, o2, l, tile, 0)

    @pl.loop(0, 2)
    def _(m):
        for w, tile in enumerate(row_tiles + (t,)):
            pm1[m, w] = mover_matrix(s1, o1, m, tile, 1)

    lower = lax.broadcasted_iota(jnp.int32, (W, W), 0) >= lax.broadcasted_iota(jnp.int32, (W, W), 1)

    half = W // 2

    def pieces(ref, recv):
        return (
            (ref.at[:half, :half], recv.at[0]),
            (ref.at[half : half + half // 2], recv.at[1]),
            (ref.at[half + half // 2 :], recv.at[2]),
        )

    def clear_upper(ref):
        ref[:half, half:] = jnp.zeros((half, half), F32)

    def fan_out(who, ref, recv, root_zl, ch):
        arrive(who & ((y != 0) | (zl != root_zl)), ref, recv)
        for at, other in TREES[root_zl]:
            send(who & (y == 0) & (zl == at), ref, ref, recv, lambda o=other: dev(x, 0, ch, 0, o))
        for other in (1, 3, 2):
            send(who & (y == 0), ref, ref, recv, lambda o=other: dev(x, 0, ch, o, zl))

    @pl.when(busy)
    def _():
        inverse_factor(a2.at[0], li)

    pl.semaphore_wait(barrier, 12 + jnp.minimum(zl, 3) + jnp.minimum(7 - zl, 3))

    send((zh == 0) & (c == 1) & (x % 2 == 1), a2.at[0], pa, r_pa, lambda: dev(x - 1, zh, c, y, zl))
    exchange(jnp.logical_not(late | busy))
    pass_on(jnp.logical_not(late | busy))

    @pl.when(jnp.logical_not(is_pd0 & (t == 0)))
    def _():
        clear_upper(li)

    for part, recv in pieces(li, r_li):
        fan_out(is_pd0, part, recv, 0, 0)

    exchange(busy)
    pass_on(busy)

    @pl.when(is_pd0)
    def _():
        panel = solve_panel(a2[0], li[...])
        cb[x] = jnp.where(lower | (t != 0), panel, 0.0).astype(BF16)

    def column_stage(k, holder, own, known):
        arrive(mover & jnp.logical_not(own), cb.at[k], r_cb.at[k])
        send(mover & jnp.logical_not(known), cb.at[k], cb.at[k], r_cb.at[k], lambda: dev(x, zh, 1 - c, y, zl))
        for apart in (1, 3, 2):
            send(mover & holder, cb.at[k], cb.at[k], r_cb.at[k], lambda a=apart: dev((x + a) % 4, zh, c, y, zl))

    def line(r):
        return mover & (y == x // 2 + 2 * r)

    def halves(k, ref, recv):
        if k in (4, 5):
            return ((ref.at[:half], recv.at[0]), (ref.at[half:], recv.at[1]))
        return ((ref, recv.at[0]),)

    def row_stage(k):
        z0 = 4 * (x % 2) + 2 * zh
        for cc in range(2):
            for r in range(2):
                at = z0 + cc
                source = line(r) & (zl == at)
                ref = rb.at[k, r, cc]

                @pl.when(source)
                def _():
                    rb[k, r, cc] = cb[k]

                for part, recv in halves(k, ref, r_rb.at[k, r, cc]):
                    arrive(line(r) & (zl != at), part, recv)
                    send(line(r) & (zl >= at) & (zl < 7), part, part, recv, lambda: dev(x, zh, c, y, zl + 1))
                    send(line(r) & (zl <= at) & (zl > 0), part, part, recv, lambda: dev(x, zh, c, y, zl - 1))
                    for apart in (1, 3, 2):
                        send(line(r), part, part, recv, lambda a=apart, cc=cc: dev(x, zh, cc, (y + a) % 4, zl))
                    send(line(r) & (c != cc), part, part, recv, lambda: dev(x, zh, 1 - c, y, zl))

    def rows_here(k):
        for r in range(2):
            for part, recv in halves(k, rb.at[k, r, c], r_rb.at[k, r, c]):
                arrive(jnp.logical_not(line(r)), part, recv)

    for l in range(4):
        send(is_pd0 & (x == l), cb.at[l], cb.at[l], r_cb.at[l], lambda: dev(x, 1, 1, y, zl))
    for l in range(4):
        column_stage(l, x == l, is_pd0 & (x == l), always & False)
    def root_tiles(who):
        for l in range(4):
            for r in range(2):
                arrive(who & (x != l), ta2.at[l, r], r_ta2.at[l, r])
        for m in range(2):
            for r in range(2):
                arrive(who & (x // 2 != m), ta1.at[m, r], r_ta1.at[m, r])

        @pl.when(who)
        def _():
            @pl.loop(0, 2)
            def _(r):
                ts[0] = ta1[0, r]
                ts[1] = ta1[1, r]

                @pl.loop(0, 4)
                def _(l):
                    ts[l // 2] += place(pl2[l, r], ta2[l, r], pl2[l, 2])

                acc[r] = a0[r]

                @pl.loop(0, 2)
                def _(m):
                    acc[r] += place(pm1[m, r], ts[m], pm1[m, 2])

    exchange(late)
    pass_on(late & jnp.logical_not(mover))
    early = (zh == 1) & (c == 0)
    root_tiles(early)

    @pl.when(is_pd2)
    def _():
        high = acc[0].astype(BF16)
        cb[6] = high
        cb[7] = (acc[0] - high.astype(F32)).astype(BF16)

    for k in (6, 7):
        send(is_pd2, cb.at[k], cb.at[k], r_cb.at[k], lambda: dev(0, 1, 1, y, zl))
        send(is_pd2, cb.at[k], cb.at[k], r_cb.at[k], lambda: dev(0, 0, 0, y, zl))

    def carried(m, w, block):
        return dot(pm1[m, w], block, 1, 0).astype(BF16)

    def column_of(k):
        if k < 4:
            return carried(k // 2, 2, dot(pl2[k, 2], cb[k], 1, 0).astype(BF16))
        return carried(k - 4, 2, cb[k])

    def pivot_stage(k):
        @pl.when(mover & (t == 2))
        def _():
            vb[k] = column_of(k)

        zero = mover & (y == 0)
        arrive(zero & (zl != 2), vb.at[k], r_vb.at[k])
        send(zero & (zl >= 2) & (zl < 7), vb.at[k], vb.at[k], r_vb.at[k], lambda: dev(x, zh, c, y, zl + 1))
        send(zero & (zl <= 2) & (zl > 0), vb.at[k], vb.at[k], r_vb.at[k], lambda: dev(x, zh, c, y, zl - 1))
        for other in (1, 3, 2):
            send(zero, vb.at[k], vb.at[k], r_vb.at[k], lambda o=other: dev(x, zh, c, o, zl))
        send(zero, vb.at[k], vb.at[k], r_vb.at[k], lambda: dev(x, zh, 1 - c, y, zl))

    for l in range(4):
        arrive(jnp.logical_not(mover), cb.at[l], r_cb.at[l])

    arrive(is_pd1, pa, r_pa)

    @pl.when(is_pd1)
    def _():
        total = a1[0]
        for i in range(2):
            block = a2[0] if i == 0 else pa[...]
            left = mover_matrix(s2, o2, x + i, 1, 0)
            total = total + place(left, block, pl2[x + i, 2])
        hs[...] = total

        @pl.when(t == 1)
        def _():
            for i in range(2):
                yb[i] = dot(pl2[x + i, 2], cb[x + i], 1, 0).astype(BF16)

    for i in range(2):
        fan_out(is_pd1, yb.at[i], r_yb.at[i], 1, 1)

    @pl.when(is_pd1)
    def _():
        total = hs[...]
        for i in range(2):
            mine = dot(pl2[x + i, 2], cb[x + i], 1, 0).astype(BF16)
            total = total - dot(yb[i], mine, 1, 1)
        hs[...] = total

        @pl.when(t == 1)
        def _():
            inverse_factor(hs, l1i)

    @pl.when(jnp.logical_not(is_pd1 & (t == 1)))
    def _():
        clear_upper(l1i)

    for part, recv in pieces(l1i, r_l1):
        fan_out(is_pd1, part, recv, 1, 1)

    @pl.when(is_pd1)
    def _():
        panel = solve_panel(hs[...], l1i[...])
        cb[4 + x // 2] = jnp.where(lower | (t != 1), panel, 0.0).astype(BF16)

    for m in range(2):
        mine = is_pd1 & (x == 2 * m)
        send(mine, cb.at[4 + m], cb.at[4 + m], r_cb.at[4 + m], lambda: dev(x, 0, 0, y, zl))
        send(mine, cb.at[4 + m], cb.at[4 + m], r_cb.at[4 + m], lambda: dev(x, 1, 1, y, zl))

    hop = is_pd1 & (t == 2)
    send(hop & (x == 2), cb.at[5], vx.at[1], r_vx.at[1], lambda: dev(0, 0, 1, y, zl))
    send(hop & (x == 0), cb.at[4], vx.at[0], r_vx.at[0], lambda: dev(0, 1, 0, y, zl))
    arrive(hop & (x == 0), vx.at[1], r_vx.at[1])
    send(hop & (x == 0), vx.at[1], vx.at[1], r_vx.at[1], lambda: dev(0, 1, 0, y, zl))
    root_tiles(jnp.logical_not(early | mover))

    root = is_pd2 & (t == 2)

    for i in range(2):
        arrive(root, vx.at[i], r_vx.at[i])

    @pl.when(root)
    def _():
        total = acc[0]
        for k in range(6):
            block = column_of(k) if k < 4 else carried(k - 4, 2, vx[k - 4])
            total = total - dot(block, block, 1, 1)
        hs[...] = total
        inverse_factor(hs, l0i)

    @pl.when(jnp.logical_not(root))
    def _():
        clear_upper(l0i)

    still = jnp.logical_not(mover)
    two = still & (y == 0) & (zl == 2)
    for part, recv in pieces(l0i, r_l0):
        arrive(still & jnp.logical_not(root), part, recv)
        send(two & (x == 0) & (zh == 1), part, part, recv, lambda: dev(0, 0, 1, 0, 2))
        for other in (1, 3, 2):
            send(two & (x == 0), part, part, recv, lambda o=other: dev(o, zh, c, 0, 2))
        for other in (1, 3, 2):
            send(two, part, part, recv, lambda o=other: dev(x, zh, c, o, 2))
        for at, other in TREES[2]:
            send(still & (zl == at), part, part, recv, lambda o=other: dev(x, zh, c, y, o))
        send(still, part, part, recv, lambda: dev(x, zh, 1 - c, y, zl))

    for k in (6, 7):
        column_stage(k, x == 0, always & False, (zh == 1) & (x == 0))
    for k in (6, 7):
        row_stage(k)
    for l in range(4):
        row_stage(l)
    for l in range(4):
        pivot_stage(l)
    pass_on(late & mover)
    ahead = mover & jnp.logical_not(line(0) | line(1) | late)
    root_tiles(ahead)
    for m in range(2):
        column_stage(4 + m, x == 2 * m, always & False, (zh == 0) & (x == 2 * m))
    for m in range(2):
        arrive(jnp.logical_not(mover) & jnp.logical_not(is_pd1 & (x == 2 * m)), cb.at[4 + m], r_cb.at[4 + m])

    for m in range(2):
        row_stage(4 + m)
    for m in range(2):
        pivot_stage(4 + m)
    root_tiles(mover & jnp.logical_not(ahead))
    for k in range(6):
        arrive(mover & (y != 0), vb.at[k], r_vb.at[k])
        send(mover & (y != 0), vb.at[k], vb.at[k], r_vb.at[k], lambda: dev(x, zh, 1 - c, y, zl))
    for l in range(4):
        rows_here(l)
    for k in range(4):
        arrive(jnp.logical_not(mover), vb.at[k], r_vb.at[k])

    pick = (
        lax.broadcasted_iota(jnp.int32, (8, W), 0) + 8 * t == lax.broadcasted_iota(jnp.int32, (8, W), 1)
    )
    pick = jnp.where(pick, 1.0, 0.0).astype(BF16)

    hp[...] = jnp.zeros_like(hp)

    @pl.loop(0, 4)
    def _(l):
        m = l // 2
        col = carried(m, 2, dot(pl2[l, 2], cb[l], 1, 0).astype(BF16))
        for r in range(2):
            psend[l, r] = dot(pick, rb[l, r, c], 1, 0)
            row = carried(m, r, dot(pl2[l, r], rb[l, r, c], 1, 0).astype(BF16))
            acc[r] -= dot(row, col, 1, 1)
            hp[r] -= dot(vb[l], row, 1, 1)
        hp[2] -= dot(vb[l], col, 1, 1)

    for apart in (1, 3, 2):
        xd = (x + apart) % 4
        send(always, psend.at[xd], precv.at[x], r_ps.at[x], lambda xd=xd: dev(xd, zh, c, y, zl))
    precv[x] = psend[x]

    for m in range(2):
        rows_here(4 + m)
        arrive(jnp.logical_not(mover), vb.at[4 + m], r_vb.at[4 + m])

    @pl.loop(0, 2)
    def _(m):
        col = carried(m, 2, cb[4 + m])
        for r in range(2):
            msend[m, r] = dot(pick, rb[4 + m, r, c], 1, 0)
            row = carried(m, r, rb[4 + m, r, c])
            acc[r] -= dot(row, col, 1, 1)
            hp[r] -= dot(vb[4 + m], row, 1, 1)
        hp[2] -= dot(vb[4 + m], col, 1, 1)

    send(always, msend.at[xo // 2], mrecv.at[x // 2], r_ms.at[x // 2], lambda: dev(xo, zh, c, y, zl))
    mrecv[x // 2] = msend[x // 2]

    for k in (6, 7):
        arrive(jnp.logical_not(mover) & jnp.logical_not(is_pd2), cb.at[k], r_cb.at[k])
        rows_here(k)

    for part, recv in pieces(l0i, r_l0):
        arrive(mover, part, recv)

    def last_panel(w, high, low):
        return solve_panel(hp[w] + high.astype(F32) + low.astype(F32), l0i[...])

    col = last_panel(2, cb[6], cb[7])
    col = jnp.where(t == 2, 0.0, col).astype(BF16)
    for r in range(2):
        tile = row_tiles[r]
        full = last_panel(r, rb[6, r, c], rb[7, r, c])
        full = jnp.where(lower | (tile != 2), full, 0.0).astype(BF16)
        root_out[r, 0] = dot(pick, full, 1, 0).astype(BF16)
        row = jnp.where(tile == 2, jnp.zeros_like(full), full)
        schur_out[r] = (acc[r] - dot(row, col, 1, 1)).astype(BF16)

    for s in range(4):
        arrive(x != s, precv.at[s], r_ps.at[s])
    for s in range(2):
        arrive(x // 2 != s, mrecv.at[s], r_ms.at[s])
    for s in range(4):
        for r in range(2):
            leaf_out[4 * r + s, 0] = precv[s, r].astype(BF16)
    for s in range(2):
        for r in range(2):
            mid_out[2 * r + s, 0] = mrecv[s, r].astype(BF16)

    for pred, make in pending:

        @pl.when(pred)
        def _(make=make):
            make().wait_send()


def per_device(leaf, middle, root, s2, s1, o2, o1):
    vmem = pl.BlockSpec(memory_space=pltpu.VMEM)
    smem = pl.BlockSpec(memory_space=pltpu.SMEM)
    dma = pltpu.SemaphoreType.DMA
    outs = [
        jax.ShapeDtypeStruct((8, 1, 8, W), BF16),
        jax.ShapeDtypeStruct((4, 1, 8, W), BF16),
        jax.ShapeDtypeStruct((2, 1, 8, W), BF16),
        jax.ShapeDtypeStruct((2, W, W), BF16),
    ]
    tile = (W, W)
    scratch = [
        pltpu.VMEM((4, 2) + tile, F32),
        pltpu.VMEM((2, 2) + tile, F32),
        pltpu.VMEM(tile, F32),
        pltpu.VMEM((8,) + tile, BF16),
        pltpu.VMEM((8, 2, 2) + tile, BF16),
        pltpu.VMEM(tile, F32),
        pltpu.VMEM((2,) + tile, BF16),
        pltpu.VMEM(tile, F32),
        pltpu.VMEM(tile, F32),
        pltpu.VMEM(tile, F32),
        pltpu.VMEM((4, 3) + tile, BF16),
        pltpu.VMEM((2, 3) + tile, BF16),
        pltpu.VMEM((2,) + tile, F32),
        pltpu.VMEM((2,) + tile, F32),
        pltpu.VMEM((4, 2, 8, W), F32),
        pltpu.VMEM((4, 2, 8, W), F32),
        pltpu.VMEM((2, 2, 8, W), F32),
        pltpu.VMEM((2, 2, 8, W), F32),
        pltpu.VMEM((2, 2) + tile, F32),
        pltpu.VMEM((6,) + tile, BF16),
        pltpu.VMEM((3,) + tile, F32),
        pltpu.VMEM((2,) + tile, BF16),
        dma((SENDS,)),
        dma((4, 2)), dma((2, 2)), dma, dma((8,)), dma((8, 2, 2, 2)),
        dma((3,)), dma((2,)), dma((3,)), dma((3,)), dma((4,)), dma((2,)), dma((2, 2)), dma((6,)), dma((2,)),
    ]
    *panels, schur = pl.pallas_call(
        kernel,
        out_shape=outs,
        in_specs=[vmem] * 5 + [smem] * 2,
        out_specs=[vmem] * 4,
        scratch_shapes=scratch,
        compiler_params=pltpu.CompilerParams(has_side_effects=True, collective_id=0, vmem_limit_bytes=60 * 2**20),
        name="window",
    )(leaf.reshape(8, W, W), middle.reshape(4, W, W), root.reshape(2, W, W), s2, s1, o2, o1)
    return (*panels, schur.reshape(2, W, 1, W))


SENDS = 560


def solution(mesh):
    return jax.shard_map(
        per_device,
        mesh=mesh,
        in_specs=(P(None, "cube", None, "tile"),) * 3 + (P(),) * 4,
        out_specs=(P(None, "cube", "tile", None),) * 3 + (P(None, "cube", None, "tile"),),
        check_vma=False,
    )
```

```python
import jax
import jax.numpy as jnp
from jax import lax
from jax.experimental import pallas as pl
from jax.experimental.pallas import tpu as pltpu
from jax.sharding import PartitionSpec as P

MESH = pl.DeviceIdType.MESH
HIGHEST = lax.Precision.HIGHEST
F32, BF16 = jnp.float32, jnp.bfloat16
W = 256
TREES = (
    ((0, 3), (0, 1), (3, 5), (3, 4), (1, 2), (5, 7), (5, 6)),
    ((1, 4), (1, 2), (1, 0), (4, 6), (4, 5), (2, 3), (6, 7)),
    ((2, 5), (2, 3), (2, 1), (5, 7), (5, 6), (3, 4), (1, 0)),
)


def dot(a, b, ca, cb, precision=None):
    return lax.dot_general(
        a, b, (((ca,), (cb,)), ((), ())), precision=precision, preferred_element_type=F32
    )


def inverse_factor_128(a):
    n = a.shape[0]
    rows = lax.broadcasted_iota(jnp.int32, (n, 1), 0)
    first = lax.broadcasted_iota(jnp.int32, (8, 1), 0)
    eye = lax.broadcasted_iota(jnp.int32, (n, n), 0) == lax.broadcasted_iota(jnp.int32, (n, n), 1)

    def trip(block, ab):
        a, b = ab
        live = rows < n - 8 * block
        pivots = jnp.ones((8, 1), F32)
        for i in range(8):
            row_a, row_b = a[i : i + 1, :], b[i : i + 1, :]
            pivot = a[i : i + 1, i : i + 1]
            pivots = jnp.where(first == i, pivot, pivots)
            scale = jnp.where(live & (rows > i), a[:, i : i + 1] * (1.0 / pivot), 0.0)
            a = a - scale * row_a
            b = b - scale * row_b
        b = jnp.concatenate([b[8:], b[:8] * lax.rsqrt(pivots)], 0)
        a = pltpu.roll(jnp.concatenate([a[8:], a[:8]], 0), n - 8, 1)
        return a, b

    return lax.fori_loop(0, n // 8, trip, (a, eye.astype(F32)))[1]


def inverse_factor(source, target):
    h = W // 2
    i11 = inverse_factor_128(source[:h, :h])
    l21 = dot(source[h:, :h], i11, 1, 1, HIGHEST)
    i22 = inverse_factor_128(source[h:, h:] - dot(l21, l21, 1, 1, HIGHEST))
    i21 = -dot(i22, dot(l21, i11, 1, 0, HIGHEST), 1, 0, HIGHEST)
    target[:h, :h] = i11
    target[:h, h:] = jnp.zeros((h, h), F32)
    target[h:, :h] = i21
    target[h:, h:] = i22


def solve_panel(row_block, inverse):
    return dot(row_block, inverse, 0, 1, HIGHEST)


def place(left, block, right):
    high = block.astype(BF16)
    low = (block - high.astype(F32)).astype(BF16)
    total = None
    for part in (high, low):
        moved = dot(left, part, 1, 0).astype(BF16)
        moved = dot(moved, right, 1, 1)
        total = moved if total is None else total + moved
    return total


def kernel(
    a2, a1, a0, s2, s1, o2, o1,
    leaf_out, mid_out, root_out, schur_out,
    ta2, ta1, pa, cb, rb, li, yb, l1i, l0i, hs, pl2, pm1, acc, ts, psend, precv, msend, mrecv, rel, vb, hp, vx,
    send_sem, r_ta2, r_ta1, r_pa, r_cb, r_rb, r_li, r_yb, r_l1, r_l0, r_ps, r_ms, r_rel, r_vb, r_vx,
):
    cube, t = lax.axis_index("cube"), lax.axis_index("tile")
    x, zh, c = cube // 4, (cube // 2) % 2, cube % 2
    y, zl = t // 8, t % 8
    g = 2 * zh + c
    mover = c == zh
    still = c != zh
    pending = []

    def dev(x_, zh_, c_, y_, zl_):
        return (x_ * 4 + zh_ * 2 + c_, y_ * 8 + zl_)

    def send(pred, src, dst, recv, target):
        index = len(pending)

        def make():
            return pltpu.make_async_remote_copy(
                src_ref=src, dst_ref=dst, send_sem=send_sem.at[index], recv_sem=recv,
                device_id=target(), device_id_type=MESH,
            )

        assert index < SENDS
        pending.append((pred, make))

        @pl.when(pred)
        def _():
            make().start()

    def arrive(pred, dst, recv):
        @pl.when(pred)
        def _():
            pltpu.make_async_remote_copy(
                src_ref=dst, dst_ref=dst, send_sem=send_sem.at[0], recv_sem=recv,
                device_id=(cube, t), device_id_type=MESH,
            ).wait_recv()

    always = x >= 0
    is_pd0 = (zh == 0) & (c == 0)
    is_pd1 = (zh == 0) & (c == 1) & (x % 2 == 0)
    is_pd2 = (x == 0) & (zh == 1) & (c == 0)

    xo = (x + 2) % 4

    def exchange(who):
        for step in (1, 3):
            xd = (x + step) % 4
            r = step // 2
            for j, src in ((0, a2.at[4 * r + xo]), (1, a1.at[2 * r + xo // 2])):
                send(who, src, rel.at[r, j], r_rel.at[r, j], lambda xd=xd: dev(xd, zh, c, y, zl))
        for step in (1, 3):
            xd = (x + step) % 4
            for r in range(2):
                send(who, a2.at[4 * r + xd], ta2.at[x, r], r_ta2.at[x, r], lambda xd=xd: dev(xd, zh, c, y, zl))

    def pass_on(who):
        for step in (1, 3):
            xd, xs = (x + step) % 4, (x + 4 - step) % 4
            r = step // 2
            for j, dst, recv in ((0, ta2.at[xs, r], r_ta2.at[xs, r]), (1, ta1.at[xs // 2, r], r_ta1.at[xs // 2, r])):
                arrive(who, rel.at[r, j], r_rel.at[r, j])
                send(who, rel.at[r, j], dst, recv, lambda xd=xd: dev(xd, zh, c, y, zl))

    late = t == 1
    busy = is_pd0 & (t == 0)

    barrier = pltpu.get_barrier_semaphore()

    def signal(target):
        pl.semaphore_signal(barrier, inc=1, device_id=target, device_id_type=MESH)

    for apart in (1, 2, 3):
        signal(dev((x + apart) % 4, zh, c, y, zl))
        for cc in range(2):
            signal(dev(x, zh, cc, (y + apart) % 4, zl))
    signal(dev(x, zh, 1 - c, y, zl))
    for cc in range(2):
        signal(dev(x, 1 - zh, cc, y, zl))
    for apart in (-3, -2, -1, 1, 2, 3):

        @pl.when((zl + apart >= 0) & (zl + apart < 8))
        def _(apart=apart):
            signal(dev(x, zh, c, y, zl + apart))

    for r in range(2):
        ta2[x, r] = a2[4 * r + x]
        ta1[x // 2, r] = a1[2 * r + x // 2]

    slot = lax.broadcasted_iota(jnp.int32, (W, W), 0)
    offset = lax.broadcasted_iota(jnp.int32, (1, W), 1)

    def mover_matrix(table, orders, front, tile, pivot):
        keep = (tile * W + offset < orders[front]) & (tile != pivot)
        hit = (table[front, pl.ds(tile, 1), :] == slot) & keep
        return jnp.where(hit, 1.0, 0.0).astype(BF16)

    row_tiles = (4 * x + g, 4 * x + g + 16)

    @pl.loop(0, 4)
    def _(l):
        for w, tile in enumerate(row_tiles + (t,)):
            pl2[l, w] = mover_matrix(s2, o2, l, tile, 0)

    @pl.loop(0, 2)
    def _(m):
        for w, tile in enumerate(row_tiles + (t,)):
            pm1[m, w] = mover_matrix(s1, o1, m, tile, 1)

    lower = lax.broadcasted_iota(jnp.int32, (W, W), 0) >= lax.broadcasted_iota(jnp.int32, (W, W), 1)

    half = W // 2

    def pieces(ref, recv):
        return (
            (ref.at[:half, :half], recv.at[0]),
            (ref.at[half : half + half // 2], recv.at[1]),
            (ref.at[half + half // 2 :], recv.at[2]),
        )

    def clear_upper(ref):
        ref[:half, half:] = jnp.zeros((half, half), F32)

    def fan_out(who, ref, recv, root_zl, ch):
        arrive(who & ((y != 0) | (zl != root_zl)), ref, recv)
        for at, other in TREES[root_zl]:
            send(who & (y == 0) & (zl == at), ref, ref, recv, lambda o=other: dev(x, 0, ch, 0, o))
        for other in (1, 3, 2):
            send(who & (y == 0), ref, ref, recv, lambda o=other: dev(x, 0, ch, o, zl))

    @pl.when(busy)
    def _():
        inverse_factor(a2.at[0], li)

    pl.semaphore_wait(barrier, 12 + jnp.minimum(zl, 3) + jnp.minimum(7 - zl, 3))

    send((zh == 0) & (c == 1) & (x % 2 == 1), a2.at[0], pa, r_pa, lambda: dev(x - 1, zh, c, y, zl))
    exchange(jnp.logical_not(late | busy))
    pass_on(jnp.logical_not(late | busy))

    @pl.when(jnp.logical_not(is_pd0 & (t == 0)))
    def _():
        clear_upper(li)

    for part, recv in pieces(li, r_li):
        fan_out(is_pd0, part, recv, 0, 0)

    exchange(busy)
    pass_on(busy)

    @pl.when(is_pd0)
    def _():
        panel = solve_panel(a2[0], li[...])
        cb[x] = jnp.where(lower | (t != 0), panel, 0.0).astype(BF16)

    def carrier(k):
        return still if k in (4, 5) else mover

    def column_stage(k, holder, own, known):
        arrive(carrier(k) & jnp.logical_not(own), cb.at[k], r_cb.at[k])
        send(carrier(k) & jnp.logical_not(known), cb.at[k], cb.at[k], r_cb.at[k], lambda: dev(x, zh, 1 - c, y, zl))
        for apart in (1, 3, 2):
            send(carrier(k) & holder, cb.at[k], cb.at[k], r_cb.at[k], lambda a=apart: dev((x + a) % 4, zh, c, y, zl))

    def line(r, k=0):
        return carrier(k) & (y == x // 2 + 2 * r)

    def halves(k, ref, recv):
        if k in (4, 5):
            return ((ref.at[:half], recv.at[0]), (ref.at[half:], recv.at[1]))
        return ((ref, recv.at[0]),)

    def row_stage(k):
        z0 = 4 * (x % 2) + 2 * zh
        for cc in range(2):
            for r in range(2):
                at = z0 + cc
                source = line(r, k) & (zl == at)
                ref = rb.at[k, r, cc]

                @pl.when(source)
                def _():
                    rb[k, r, cc] = cb[k]

                for part, recv in halves(k, ref, r_rb.at[k, r, cc]):
                    arrive(line(r, k) & (zl != at), part, recv)
                    send(line(r, k) & (zl >= at) & (zl < 7), part, part, recv, lambda: dev(x, zh, c, y, zl + 1))
                    send(line(r, k) & (zl <= at) & (zl > 0), part, part, recv, lambda: dev(x, zh, c, y, zl - 1))
                    for apart in (1, 3, 2):
                        send(line(r, k), part, part, recv, lambda a=apart, cc=cc: dev(x, zh, cc, (y + a) % 4, zl))
                    send(line(r, k) & (c != cc), part, part, recv, lambda: dev(x, zh, 1 - c, y, zl))

    def rows_here(k):
        for r in range(2):
            for part, recv in halves(k, rb.at[k, r, c], r_rb.at[k, r, c]):
                arrive(jnp.logical_not(line(r, k)), part, recv)

    for l in range(4):
        send(is_pd0 & (x == l), cb.at[l], cb.at[l], r_cb.at[l], lambda: dev(x, 1, 1, y, zl))
    for l in range(4):
        column_stage(l, x == l, is_pd0 & (x == l), always & False)
    def root_tiles(who):
        for l in range(4):
            for r in range(2):
                arrive(who & (x != l), ta2.at[l, r], r_ta2.at[l, r])
        for m in range(2):
            for r in range(2):
                arrive(who & (x // 2 != m), ta1.at[m, r], r_ta1.at[m, r])

        @pl.when(who)
        def _():
            @pl.loop(0, 2)
            def _(r):
                ts[0] = ta1[0, r]
                ts[1] = ta1[1, r]

                @pl.loop(0, 4)
                def _(l):
                    ts[l // 2] += place(pl2[l, r], ta2[l, r], pl2[l, 2])

                acc[r] = a0[r]

                @pl.loop(0, 2)
                def _(m):
                    acc[r] += place(pm1[m, r], ts[m], pm1[m, 2])

    exchange(late)
    pass_on(late & jnp.logical_not(mover))
    early = (zh == 1) & (c == 0)
    root_tiles(early)

    @pl.when(is_pd2)
    def _():
        high = acc[0].astype(BF16)
        cb[6] = high
        cb[7] = (acc[0] - high.astype(F32)).astype(BF16)

    for k in (6, 7):
        send(is_pd2, cb.at[k], cb.at[k], r_cb.at[k], lambda: dev(0, 1, 1, y, zl))
        send(is_pd2, cb.at[k], cb.at[k], r_cb.at[k], lambda: dev(0, 0, 0, y, zl))

    def carried(m, w, block):
        return dot(pm1[m, w], block, 1, 0).astype(BF16)

    def column_of(k):
        if k < 4:
            return carried(k // 2, 2, dot(pl2[k, 2], cb[k], 1, 0).astype(BF16))
        return carried(k - 4, 2, cb[k])

    def pivot_stage(k):
        @pl.when(carrier(k) & (t == 2))
        def _():
            vb[k] = column_of(k)

        zero = carrier(k) & (y == 0)
        arrive(zero & (zl != 2), vb.at[k], r_vb.at[k])
        send(zero & (zl >= 2) & (zl < 7), vb.at[k], vb.at[k], r_vb.at[k], lambda: dev(x, zh, c, y, zl + 1))
        send(zero & (zl <= 2) & (zl > 0), vb.at[k], vb.at[k], r_vb.at[k], lambda: dev(x, zh, c, y, zl - 1))
        for other in (1, 3, 2):
            send(zero, vb.at[k], vb.at[k], r_vb.at[k], lambda o=other: dev(x, zh, c, o, zl))
        send(zero, vb.at[k], vb.at[k], r_vb.at[k], lambda: dev(x, zh, 1 - c, y, zl))

    for l in range(4):
        arrive(jnp.logical_not(mover), cb.at[l], r_cb.at[l])

    arrive(is_pd1, pa, r_pa)

    @pl.when(is_pd1)
    def _():
        total = a1[0]
        for i in range(2):
            block = a2[0] if i == 0 else pa[...]
            left = mover_matrix(s2, o2, x + i, 1, 0)
            total = total + place(left, block, pl2[x + i, 2])
        hs[...] = total

        @pl.when(t == 1)
        def _():
            for i in range(2):
                yb[i] = dot(pl2[x + i, 2], cb[x + i], 1, 0).astype(BF16)

    for i in range(2):
        fan_out(is_pd1, yb.at[i], r_yb.at[i], 1, 1)

    @pl.when(is_pd1)
    def _():
        total = hs[...]
        for i in range(2):
            mine = dot(pl2[x + i, 2], cb[x + i], 1, 0).astype(BF16)
            total = total - dot(yb[i], mine, 1, 1)
        hs[...] = total

        @pl.when(t == 1)
        def _():
            inverse_factor(hs, l1i)

    @pl.when(jnp.logical_not(is_pd1 & (t == 1)))
    def _():
        clear_upper(l1i)

    for part, recv in pieces(l1i, r_l1):
        fan_out(is_pd1, part, recv, 1, 1)

    @pl.when(is_pd1)
    def _():
        panel = solve_panel(hs[...], l1i[...])
        cb[4 + x // 2] = jnp.where(lower | (t != 1), panel, 0.0).astype(BF16)

    for m in range(2):
        mine = is_pd1 & (x == 2 * m)
        send(mine, cb.at[4 + m], cb.at[4 + m], r_cb.at[4 + m], lambda: dev(x, 1, 0, y, zl))

    hop = is_pd1 & (t == 2)
    send(hop & (x == 2), cb.at[5], vx.at[1], r_vx.at[1], lambda: dev(0, 0, 1, y, zl))
    send(hop & (x == 0), cb.at[4], vx.at[0], r_vx.at[0], lambda: dev(0, 1, 0, y, zl))
    arrive(hop & (x == 0), vx.at[1], r_vx.at[1])
    send(hop & (x == 0), vx.at[1], vx.at[1], r_vx.at[1], lambda: dev(0, 1, 0, y, zl))
    root_tiles(jnp.logical_not(early | mover))

    root = is_pd2 & (t == 2)

    for i in range(2):
        arrive(root, vx.at[i], r_vx.at[i])

    @pl.when(root)
    def _():
        total = acc[0]
        for k in range(6):
            block = column_of(k) if k < 4 else carried(k - 4, 2, vx[k - 4])
            total = total - dot(block, block, 1, 1)
        hs[...] = total
        inverse_factor(hs, l0i)

    @pl.when(jnp.logical_not(root))
    def _():
        clear_upper(l0i)

    for k in (6, 7):
        column_stage(k, x == 0, always & False, (zh == 1) & (x == 0))
    for k in (6, 7):
        row_stage(k)
    for l in range(4):
        row_stage(l)
    for l in range(4):
        pivot_stage(l)
    pass_on(late & mover)
    root_tiles(mover & jnp.logical_not(late))
    two = mover & (y == 0) & (zl == 2)
    for part, recv in pieces(l0i, r_l0):
        send(root, part, part, recv, lambda: dev(0, 1, 1, 0, 2))
        arrive(mover, part, recv)
        send(two & (x == 0) & (zh == 1), part, part, recv, lambda: dev(0, 0, 0, 0, 2))
        for other in (1, 3, 2):
            send(two & (x == 0), part, part, recv, lambda o=other: dev(o, zh, c, 0, 2))
        for other in (1, 3, 2):
            send(two, part, part, recv, lambda o=other: dev(x, zh, c, o, 2))
        for at, other in TREES[2]:
            send(mover & (zl == at), part, part, recv, lambda o=other: dev(x, zh, c, y, o))
        send(
            mover & jnp.logical_not((x == 0) & (zh == 1) & (t == 2)),
            part, part, recv, lambda: dev(x, zh, 1 - c, y, zl),
        )
    root_tiles(mover & late)
    for m in range(2):
        column_stage(4 + m, x == 2 * m, is_pd1 & (x == 2 * m), always & False)
    for m in range(2):
        row_stage(4 + m)
    for m in range(2):
        pivot_stage(4 + m)
    for k in range(6):
        relay = carrier(k) & (y != 0)
        arrive(relay, vb.at[k], r_vb.at[k])
        send(relay, vb.at[k], vb.at[k], r_vb.at[k], lambda: dev(x, zh, 1 - c, y, zl))
    for l in range(4):
        rows_here(l)
    for k in range(4):
        arrive(jnp.logical_not(mover), vb.at[k], r_vb.at[k])

    pick = (
        lax.broadcasted_iota(jnp.int32, (8, W), 0) + 8 * t == lax.broadcasted_iota(jnp.int32, (8, W), 1)
    )
    pick = jnp.where(pick, 1.0, 0.0).astype(BF16)

    hp[...] = jnp.zeros_like(hp)

    @pl.loop(0, 4)
    def _(l):
        m = l // 2
        col = carried(m, 2, dot(pl2[l, 2], cb[l], 1, 0).astype(BF16))
        for r in range(2):
            psend[l, r] = dot(pick, rb[l, r, c], 1, 0)
            row = carried(m, r, dot(pl2[l, r], rb[l, r, c], 1, 0).astype(BF16))
            acc[r] -= dot(row, col, 1, 1)
            hp[r] -= dot(vb[l], row, 1, 1)
        hp[2] -= dot(vb[l], col, 1, 1)

    for apart in (1, 3, 2):
        xd = (x + apart) % 4
        send(always, psend.at[xd], precv.at[x], r_ps.at[x], lambda xd=xd: dev(xd, zh, c, y, zl))
    precv[x] = psend[x]

    for m in range(2):
        rows_here(4 + m)
        arrive(mover, cb.at[4 + m], r_cb.at[4 + m])
        arrive(mover, vb.at[4 + m], r_vb.at[4 + m])

    @pl.loop(0, 2)
    def _(m):
        col = carried(m, 2, cb[4 + m])
        for r in range(2):
            msend[m, r] = dot(pick, rb[4 + m, r, c], 1, 0)
            row = carried(m, r, rb[4 + m, r, c])
            acc[r] -= dot(row, col, 1, 1)
            hp[r] -= dot(vb[4 + m], row, 1, 1)
        hp[2] -= dot(vb[4 + m], col, 1, 1)

    send(always, msend.at[xo // 2], mrecv.at[x // 2], r_ms.at[x // 2], lambda: dev(xo, zh, c, y, zl))
    mrecv[x // 2] = msend[x // 2]

    for k in (6, 7):
        arrive(jnp.logical_not(mover) & jnp.logical_not(is_pd2), cb.at[k], r_cb.at[k])
        rows_here(k)

    for part, recv in pieces(l0i, r_l0):
        arrive(still & jnp.logical_not(root), part, recv)

    def last_panel(w, high, low):
        return solve_panel(hp[w] + high.astype(F32) + low.astype(F32), l0i[...])

    col = last_panel(2, cb[6], cb[7])
    col = jnp.where(t == 2, 0.0, col).astype(BF16)
    for r in range(2):
        tile = row_tiles[r]
        full = last_panel(r, rb[6, r, c], rb[7, r, c])
        full = jnp.where(lower | (tile != 2), full, 0.0).astype(BF16)
        root_out[r, 0] = dot(pick, full, 1, 0).astype(BF16)
        row = jnp.where(tile == 2, jnp.zeros_like(full), full)
        schur_out[r] = (acc[r] - dot(row, col, 1, 1)).astype(BF16)

    for s in range(4):
        arrive(x != s, precv.at[s], r_ps.at[s])
    for s in range(2):
        arrive(x // 2 != s, mrecv.at[s], r_ms.at[s])
    for s in range(4):
        for r in range(2):
            leaf_out[4 * r + s, 0] = precv[s, r].astype(BF16)
    for s in range(2):
        for r in range(2):
            mid_out[2 * r + s, 0] = mrecv[s, r].astype(BF16)

    for pred, make in pending:

        @pl.when(pred)
        def _(make=make):
            make().wait_send()


def per_device(leaf, middle, root, s2, s1, o2, o1):
    vmem = pl.BlockSpec(memory_space=pltpu.VMEM)
    smem = pl.BlockSpec(memory_space=pltpu.SMEM)
    dma = pltpu.SemaphoreType.DMA
    outs = [
        jax.ShapeDtypeStruct((8, 1, 8, W), BF16),
        jax.ShapeDtypeStruct((4, 1, 8, W), BF16),
        jax.ShapeDtypeStruct((2, 1, 8, W), BF16),
        jax.ShapeDtypeStruct((2, W, W), BF16),
    ]
    tile = (W, W)
    scratch = [
        pltpu.VMEM((4, 2) + tile, F32),
        pltpu.VMEM((2, 2) + tile, F32),
        pltpu.VMEM(tile, F32),
        pltpu.VMEM((8,) + tile, BF16),
        pltpu.VMEM((8, 2, 2) + tile, BF16),
        pltpu.VMEM(tile, F32),
        pltpu.VMEM((2,) + tile, BF16),
        pltpu.VMEM(tile, F32),
        pltpu.VMEM(tile, F32),
        pltpu.VMEM(tile, F32),
        pltpu.VMEM((4, 3) + tile, BF16),
        pltpu.VMEM((2, 3) + tile, BF16),
        pltpu.VMEM((2,) + tile, F32),
        pltpu.VMEM((2,) + tile, F32),
        pltpu.VMEM((4, 2, 8, W), F32),
        pltpu.VMEM((4, 2, 8, W), F32),
        pltpu.VMEM((2, 2, 8, W), F32),
        pltpu.VMEM((2, 2, 8, W), F32),
        pltpu.VMEM((2, 2) + tile, F32),
        pltpu.VMEM((6,) + tile, BF16),
        pltpu.VMEM((3,) + tile, F32),
        pltpu.VMEM((2,) + tile, BF16),
        dma((SENDS,)),
        dma((4, 2)), dma((2, 2)), dma, dma((8,)), dma((8, 2, 2, 2)),
        dma((3,)), dma((2,)), dma((3,)), dma((3,)), dma((4,)), dma((2,)), dma((2, 2)), dma((6,)), dma((2,)),
    ]
    *panels, schur = pl.pallas_call(
        kernel,
        out_shape=outs,
        in_specs=[vmem] * 5 + [smem] * 2,
        out_specs=[vmem] * 4,
        scratch_shapes=scratch,
        compiler_params=pltpu.CompilerParams(has_side_effects=True, collective_id=0, vmem_limit_bytes=60 * 2**20),
        name="window",
    )(leaf.reshape(8, W, W), middle.reshape(4, W, W), root.reshape(2, W, W), s2, s1, o2, o1)
    return (*panels, schur.reshape(2, W, 1, W))


SENDS = 560


def solution(mesh):
    return jax.shard_map(
        per_device,
        mesh=mesh,
        in_specs=(P(None, "cube", None, "tile"),) * 3 + (P(),) * 4,
        out_specs=(P(None, "cube", "tile", None),) * 3 + (P(None, "cube", None, "tile"),),
        check_vma=False,
    )
```

```python
import jax
import jax.numpy as jnp
from jax import lax
from jax.experimental import pallas as pl
from jax.experimental.pallas import tpu as pltpu
from jax.sharding import PartitionSpec as P

MESH = pl.DeviceIdType.MESH
HIGHEST = lax.Precision.HIGHEST
F32, BF16 = jnp.float32, jnp.bfloat16
W = 256
TREES = (
    ((0, 3), (0, 1), (3, 5), (3, 4), (1, 2), (5, 7), (5, 6)),
    ((1, 4), (1, 2), (1, 0), (4, 6), (4, 5), (2, 3), (6, 7)),
    ((2, 5), (2, 3), (2, 1), (5, 7), (5, 6), (3, 4), (1, 0)),
)


def dot(a, b, ca, cb, precision=None):
    return lax.dot_general(
        a, b, (((ca,), (cb,)), ((), ())), precision=precision, preferred_element_type=F32
    )


def inverse_factor_128(a):
    n = a.shape[0]
    rows = lax.broadcasted_iota(jnp.int32, (n, 1), 0)
    first = lax.broadcasted_iota(jnp.int32, (8, 1), 0)
    eye = lax.broadcasted_iota(jnp.int32, (n, n), 0) == lax.broadcasted_iota(jnp.int32, (n, n), 1)

    def trip(block, ab):
        a, b = ab
        live = rows < n - 8 * block
        pivots = jnp.ones((8, 1), F32)
        for i in range(8):
            row_a, row_b = a[i : i + 1, :], b[i : i + 1, :]
            pivot = a[i : i + 1, i : i + 1]
            pivots = jnp.where(first == i, pivot, pivots)
            scale = jnp.where(live & (rows > i), a[:, i : i + 1] * (1.0 / pivot), 0.0)
            a = a - scale * row_a
            b = b - scale * row_b
        b = jnp.concatenate([b[8:], b[:8] * lax.rsqrt(pivots)], 0)
        a = pltpu.roll(jnp.concatenate([a[8:], a[:8]], 0), n - 8, 1)
        return a, b

    return lax.fori_loop(0, n // 8, trip, (a, eye.astype(F32)))[1]


def inverse_factor(source, target):
    h = W // 2
    i11 = inverse_factor_128(source[:h, :h])
    l21 = dot(source[h:, :h], i11, 1, 1, HIGHEST)
    i22 = inverse_factor_128(source[h:, h:] - dot(l21, l21, 1, 1, HIGHEST))
    i21 = -dot(i22, dot(l21, i11, 1, 0, HIGHEST), 1, 0, HIGHEST)
    target[:h, :h] = i11
    target[:h, h:] = jnp.zeros((h, h), F32)
    target[h:, :h] = i21
    target[h:, h:] = i22


def solve_panel(row_block, inverse):
    return dot(row_block, inverse, 0, 1, HIGHEST)


def place(left, block, right):
    high = block.astype(BF16)
    low = (block - high.astype(F32)).astype(BF16)
    total = None
    for part in (high, low):
        moved = dot(left, part, 1, 0).astype(BF16)
        moved = dot(moved, right, 1, 1)
        total = moved if total is None else total + moved
    return total


def kernel(
    a2, a1, a0, s2, s1, o2, o1,
    leaf_out, mid_out, root_out, schur_out,
    ta2, ta1, pa, cb, rb, li, yb, l1i, l0i, hs, pl2, pm1, acc, ts, psend, precv, msend, mrecv, rel, vb, hp, vx,
    send_sem, r_ta2, r_ta1, r_pa, r_cb, r_rb, r_li, r_yb, r_l1, r_l0, r_ps, r_ms, r_rel, r_vb, r_vx,
):
    cube, t = lax.axis_index("cube"), lax.axis_index("tile")
    x, zh, c = cube // 4, (cube // 2) % 2, cube % 2
    y, zl = t // 8, t % 8
    g = 2 * zh + c
    mover = c == zh
    still = c != zh
    pending, used = {}, []

    def dev(x_, zh_, c_, y_, zl_):
        return (x_ * 4 + zh_ * 2 + c_, y_ * 8 + zl_)

    def send_all(pred, copies, outer=None):
        makers = []
        for src, dst, recv, target in copies:
            index = len(used)
            assert index < SENDS
            used.append(index)

            def make(src=src, dst=dst, recv=recv, target=target, index=index):
                return pltpu.make_async_remote_copy(
                    src_ref=src, dst_ref=dst, send_sem=send_sem.at[index], recv_sem=recv,
                    device_id=target(), device_id_type=MESH,
                )

            makers.append(make)
        pending.setdefault(outer and outer[0], (outer and outer[1], []))[1].append((pred, makers))

        @pl.when(pred)
        def _():
            for make in makers:
                make().start()

    def send(pred, src, dst, recv, target, outer=None):
        send_all(pred, [(src, dst, recv, target)], outer)

    def arrive(pred, dst, recv):
        @pl.when(pred)
        def _():
            pltpu.make_async_remote_copy(
                src_ref=dst, dst_ref=dst, send_sem=send_sem.at[0], recv_sem=recv,
                device_id=(cube, t), device_id_type=MESH,
            ).wait_recv()

    always = x >= 0
    is_pd0 = (zh == 0) & (c == 0)
    is_pd1 = (zh == 0) & (c == 1) & (x % 2 == 0)
    is_pd2 = (x == 0) & (zh == 1) & (c == 0)

    xo = (x + 2) % 4

    def exchange(who):
        for step in (1, 3):
            xd = (x + step) % 4
            r = step // 2
            for j, src in ((0, a2.at[4 * r + xo]), (1, a1.at[2 * r + xo // 2])):
                send(who, src, rel.at[r, j], r_rel.at[r, j], lambda xd=xd: dev(xd, zh, c, y, zl))
        for step in (1, 3):
            xd = (x + step) % 4
            for r in range(2):
                send(who, a2.at[4 * r + xd], ta2.at[x, r], r_ta2.at[x, r], lambda xd=xd: dev(xd, zh, c, y, zl))

    def pass_on(who):
        for step in (1, 3):
            xd, xs = (x + step) % 4, (x + 4 - step) % 4
            r = step // 2
            for j, dst, recv in ((0, ta2.at[xs, r], r_ta2.at[xs, r]), (1, ta1.at[xs // 2, r], r_ta1.at[xs // 2, r])):
                arrive(who, rel.at[r, j], r_rel.at[r, j])
                send(who, rel.at[r, j], dst, recv, lambda xd=xd: dev(xd, zh, c, y, zl))

    late = t == 1
    busy = is_pd0 & (t == 0)

    barrier = pltpu.get_barrier_semaphore()

    def signal(target):
        pl.semaphore_signal(barrier, inc=1, device_id=target, device_id_type=MESH)

    for apart in (1, 2, 3):
        signal(dev((x + apart) % 4, zh, c, y, zl))
        for cc in range(2):
            signal(dev(x, zh, cc, (y + apart) % 4, zl))
    signal(dev(x, zh, 1 - c, y, zl))
    for cc in range(2):
        signal(dev(x, 1 - zh, cc, y, zl))
    for apart in (-3, -2, -1, 1, 2, 3):

        @pl.when((zl + apart >= 0) & (zl + apart < 8))
        def _(apart=apart):
            signal(dev(x, zh, c, y, zl + apart))

    for r in range(2):
        ta2[x, r] = a2[4 * r + x]
        ta1[x // 2, r] = a1[2 * r + x // 2]

    slot = lax.broadcasted_iota(jnp.int32, (W, W), 0)
    offset = lax.broadcasted_iota(jnp.int32, (1, W), 1)

    def mover_matrix(table, orders, front, tile, pivot):
        keep = (tile * W + offset < orders[front]) & (tile != pivot)
        hit = (table[front, pl.ds(tile, 1), :] == slot) & keep
        return jnp.where(hit, 1.0, 0.0).astype(BF16)

    row_tiles = (4 * x + g, 4 * x + g + 16)

    @pl.loop(0, 4)
    def _(l):
        for w, tile in enumerate(row_tiles + (t,)):
            pl2[l, w] = mover_matrix(s2, o2, l, tile, 0)

    @pl.loop(0, 2)
    def _(m):
        for w, tile in enumerate(row_tiles + (t,)):
            pm1[m, w] = mover_matrix(s1, o1, m, tile, 1)

    lower = lax.broadcasted_iota(jnp.int32, (W, W), 0) >= lax.broadcasted_iota(jnp.int32, (W, W), 1)

    half = W // 2

    def pieces(ref, recv):
        return (
            (ref.at[:half, :half], recv.at[0]),
            (ref.at[half : half + half // 2], recv.at[1]),
            (ref.at[half + half // 2 :], recv.at[2]),
        )

    def clear_upper(ref):
        ref[:half, half:] = jnp.zeros((half, half), F32)

    def fan_out(who, ref, recv, root_zl, ch):
        arrive(who & ((y != 0) | (zl != root_zl)), ref, recv)
        for at, other in TREES[root_zl]:
            send(who & (y == 0) & (zl == at), ref, ref, recv, lambda o=other: dev(x, 0, ch, 0, o))
        send_all(who & (y == 0), [(ref, ref, recv, lambda o=other: dev(x, 0, ch, o, zl)) for other in (1, 3, 2)])

    @pl.when(busy)
    def _():
        inverse_factor(a2.at[0], li)

    pl.semaphore_wait(barrier, 12 + jnp.minimum(zl, 3) + jnp.minimum(7 - zl, 3))

    send((zh == 0) & (c == 1) & (x % 2 == 1), a2.at[0], pa, r_pa, lambda: dev(x - 1, zh, c, y, zl))
    exchange(jnp.logical_not(late | busy))
    pass_on(jnp.logical_not(late | busy))

    @pl.when(jnp.logical_not(is_pd0 & (t == 0)))
    def _():
        clear_upper(li)

    for part, recv in pieces(li, r_li):
        fan_out(is_pd0, part, recv, 0, 0)

    exchange(busy)
    pass_on(busy)

    @pl.when(is_pd0)
    def _():
        panel = solve_panel(a2[0], li[...])
        cb[x] = jnp.where(lower | (t != 0), panel, 0.0).astype(BF16)

    def carrier(k):
        return still if k in (4, 5) else mover

    def column_stage(k, holder, own, known):
        arrive(carrier(k) & jnp.logical_not(own), cb.at[k], r_cb.at[k])
        send(carrier(k) & jnp.logical_not(known), cb.at[k], cb.at[k], r_cb.at[k], lambda: dev(x, zh, 1 - c, y, zl))
        send_all(carrier(k) & holder, [(cb.at[k], cb.at[k], r_cb.at[k], lambda a=apart: dev((x + a) % 4, zh, c, y, zl)) for apart in (1, 3, 2)])

    def line(r, k=0):
        return carrier(k) & (y == x // 2 + 2 * r)

    def halves(k, ref, recv):
        if k in (4, 5):
            return ((ref.at[:half], recv.at[0]), (ref.at[half:], recv.at[1]))
        return ((ref, recv.at[0]),)

    def row_stage(k):
        z0 = 4 * (x % 2) + 2 * zh
        for cc in range(2):
            for r in range(2):
                at = z0 + cc
                source = line(r, k) & (zl == at)
                ref = rb.at[k, r, cc]

                @pl.when(source)
                def _():
                    rb[k, r, cc] = cb[k]

                outer = ((r, k in (4, 5)), line(r, k))
                for part, recv in halves(k, ref, r_rb.at[k, r, cc]):
                    arrive(line(r, k) & (zl != at), part, recv)
                    send(line(r, k) & (zl >= at) & (zl < 7), part, part, recv, lambda: dev(x, zh, c, y, zl + 1), outer)
                    send(line(r, k) & (zl <= at) & (zl > 0), part, part, recv, lambda: dev(x, zh, c, y, zl - 1), outer)
                    send_all(line(r, k), [(part, part, recv, lambda a=apart, cc=cc: dev(x, zh, cc, (y + a) % 4, zl)) for apart in (1, 3, 2)], outer)
                    send(line(r, k) & (c != cc), part, part, recv, lambda: dev(x, zh, 1 - c, y, zl), outer)

    def rows_here(k):
        for r in range(2):
            for part, recv in halves(k, rb.at[k, r, c], r_rb.at[k, r, c]):
                arrive(jnp.logical_not(line(r, k)), part, recv)

    for l in range(4):
        send(is_pd0 & (x == l), cb.at[l], cb.at[l], r_cb.at[l], lambda: dev(x, 1, 1, y, zl))
    for l in range(4):
        column_stage(l, x == l, is_pd0 & (x == l), always & False)
    def root_tiles(who):
        for l in range(4):
            for r in range(2):
                arrive(who & (x != l), ta2.at[l, r], r_ta2.at[l, r])
        for m in range(2):
            for r in range(2):
                arrive(who & (x // 2 != m), ta1.at[m, r], r_ta1.at[m, r])

        @pl.when(who)
        def _():
            @pl.loop(0, 2)
            def _(r):
                ts[0] = ta1[0, r]
                ts[1] = ta1[1, r]

                @pl.loop(0, 4)
                def _(l):
                    ts[l // 2] += place(pl2[l, r], ta2[l, r], pl2[l, 2])

                acc[r] = a0[r]

                @pl.loop(0, 2)
                def _(m):
                    acc[r] += place(pm1[m, r], ts[m], pm1[m, 2])

    exchange(late)
    pass_on(late & jnp.logical_not(mover))
    early = (zh == 1) & (c == 0)
    root_tiles(early)

    @pl.when(is_pd2)
    def _():
        high = acc[0].astype(BF16)
        cb[6] = high
        cb[7] = (acc[0] - high.astype(F32)).astype(BF16)

    for k in (6, 7):
        send(is_pd2, cb.at[k], cb.at[k], r_cb.at[k], lambda: dev(0, 1, 1, y, zl))
        send(is_pd2, cb.at[k], cb.at[k], r_cb.at[k], lambda: dev(0, 0, 0, y, zl))

    def carried(m, w, block):
        return dot(pm1[m, w], block, 1, 0).astype(BF16)

    def column_of(k):
        if k < 4:
            return carried(k // 2, 2, dot(pl2[k, 2], cb[k], 1, 0).astype(BF16))
        return carried(k - 4, 2, cb[k])

    def pivot_stage(k):
        @pl.when(carrier(k) & (t == 2))
        def _():
            vb[k] = column_of(k)

        zero = carrier(k) & (y == 0)
        arrive(zero & (zl != 2), vb.at[k], r_vb.at[k])
        send(zero & (zl >= 2) & (zl < 7), vb.at[k], vb.at[k], r_vb.at[k], lambda: dev(x, zh, c, y, zl + 1))
        send(zero & (zl <= 2) & (zl > 0), vb.at[k], vb.at[k], r_vb.at[k], lambda: dev(x, zh, c, y, zl - 1))
        send_all(zero, [(vb.at[k], vb.at[k], r_vb.at[k], lambda o=other: dev(x, zh, c, o, zl)) for other in (1, 3, 2)])
        send(zero, vb.at[k], vb.at[k], r_vb.at[k], lambda: dev(x, zh, 1 - c, y, zl))

    for l in range(4):
        arrive(jnp.logical_not(mover), cb.at[l], r_cb.at[l])

    arrive(is_pd1, pa, r_pa)

    @pl.when(is_pd1)
    def _():
        total = a1[0]
        for i in range(2):
            block = a2[0] if i == 0 else pa[...]
            left = mover_matrix(s2, o2, x + i, 1, 0)
            total = total + place(left, block, pl2[x + i, 2])
        hs[...] = total

        @pl.when(t == 1)
        def _():
            for i in range(2):
                yb[i] = dot(pl2[x + i, 2], cb[x + i], 1, 0).astype(BF16)

    for i in range(2):
        fan_out(is_pd1, yb.at[i], r_yb.at[i], 1, 1)

    @pl.when(is_pd1)
    def _():
        total = hs[...]
        for i in range(2):
            mine = dot(pl2[x + i, 2], cb[x + i], 1, 0).astype(BF16)
            total = total - dot(yb[i], mine, 1, 1)
        hs[...] = total

        @pl.when(t == 1)
        def _():
            inverse_factor(hs, l1i)

    @pl.when(jnp.logical_not(is_pd1 & (t == 1)))
    def _():
        clear_upper(l1i)

    for part, recv in pieces(l1i, r_l1):
        fan_out(is_pd1, part, recv, 1, 1)

    @pl.when(is_pd1)
    def _():
        panel = solve_panel(hs[...], l1i[...])
        cb[4 + x // 2] = jnp.where(lower | (t != 1), panel, 0.0).astype(BF16)

    for m in range(2):
        mine = is_pd1 & (x == 2 * m)
        send(mine, cb.at[4 + m], cb.at[4 + m], r_cb.at[4 + m], lambda: dev(x, 1, 0, y, zl))

    hop = is_pd1 & (t == 2)
    send(hop & (x == 2), cb.at[5], vx.at[1], r_vx.at[1], lambda: dev(0, 0, 1, y, zl))
    send(hop & (x == 0), cb.at[4], vx.at[0], r_vx.at[0], lambda: dev(0, 1, 0, y, zl))
    arrive(hop & (x == 0), vx.at[1], r_vx.at[1])
    send(hop & (x == 0), vx.at[1], vx.at[1], r_vx.at[1], lambda: dev(0, 1, 0, y, zl))
    root_tiles(jnp.logical_not(early | mover))

    root = is_pd2 & (t == 2)

    for i in range(2):
        arrive(root, vx.at[i], r_vx.at[i])

    @pl.when(root)
    def _():
        total = acc[0]
        for k in range(6):
            block = column_of(k) if k < 4 else carried(k - 4, 2, vx[k - 4])
            total = total - dot(block, block, 1, 1)
        hs[...] = total
        inverse_factor(hs, l0i)

    @pl.when(jnp.logical_not(root))
    def _():
        clear_upper(l0i)

    for k in (6, 7):
        column_stage(k, x == 0, always & False, (zh == 1) & (x == 0))
    for k in (6, 7):
        row_stage(k)
    for l in range(4):
        row_stage(l)
    for l in range(4):
        pivot_stage(l)
    pass_on(late & mover)
    root_tiles(mover & jnp.logical_not(late))
    two = mover & (y == 0) & (zl == 2)
    for part, recv in pieces(l0i, r_l0):
        send(root, part, part, recv, lambda: dev(0, 1, 1, 0, 2))
        arrive(mover, part, recv)
        send(two & (x == 0) & (zh == 1), part, part, recv, lambda: dev(0, 0, 0, 0, 2))
        send_all(two & (x == 0), [(part, part, recv, lambda o=other: dev(o, zh, c, 0, 2)) for other in (1, 3, 2)])
        send_all(two, [(part, part, recv, lambda o=other: dev(x, zh, c, o, 2)) for other in (1, 3, 2)])
        for at, other in TREES[2]:
            send(mover & (zl == at), part, part, recv, lambda o=other: dev(x, zh, c, y, o))
        send(
            mover & jnp.logical_not((x == 0) & (zh == 1) & (t == 2)),
            part, part, recv, lambda: dev(x, zh, 1 - c, y, zl),
        )
    root_tiles(mover & late)
    for m in range(2):
        column_stage(4 + m, x == 2 * m, is_pd1 & (x == 2 * m), always & False)
    for m in range(2):
        row_stage(4 + m)
    for m in range(2):
        pivot_stage(4 + m)
    for k in range(6):
        relay = carrier(k) & (y != 0)
        arrive(relay, vb.at[k], r_vb.at[k])
        send(relay, vb.at[k], vb.at[k], r_vb.at[k], lambda: dev(x, zh, 1 - c, y, zl))
    for l in range(4):
        rows_here(l)
    for k in range(4):
        arrive(jnp.logical_not(mover), vb.at[k], r_vb.at[k])

    pick = (
        lax.broadcasted_iota(jnp.int32, (8, W), 0) + 8 * t == lax.broadcasted_iota(jnp.int32, (8, W), 1)
    )
    pick = jnp.where(pick, 1.0, 0.0).astype(BF16)

    hp[...] = jnp.zeros_like(hp)

    @pl.loop(0, 4)
    def _(l):
        m = l // 2
        col = carried(m, 2, dot(pl2[l, 2], cb[l], 1, 0).astype(BF16))
        for r in range(2):
            psend[l, r] = dot(pick, rb[l, r, c], 1, 0)
            row = carried(m, r, dot(pl2[l, r], rb[l, r, c], 1, 0).astype(BF16))
            acc[r] -= dot(row, col, 1, 1)
            hp[r] -= dot(vb[l], row, 1, 1)
        hp[2] -= dot(vb[l], col, 1, 1)

    for apart in (1, 3, 2):
        xd = (x + apart) % 4
        send(always, psend.at[xd], precv.at[x], r_ps.at[x], lambda xd=xd: dev(xd, zh, c, y, zl))
    precv[x] = psend[x]

    for m in range(2):
        rows_here(4 + m)
        arrive(mover, cb.at[4 + m], r_cb.at[4 + m])
        arrive(mover, vb.at[4 + m], r_vb.at[4 + m])

    @pl.loop(0, 2)
    def _(m):
        col = carried(m, 2, cb[4 + m])
        for r in range(2):
            msend[m, r] = dot(pick, rb[4 + m, r, c], 1, 0)
            row = carried(m, r, rb[4 + m, r, c])
            acc[r] -= dot(row, col, 1, 1)
            hp[r] -= dot(vb[4 + m], row, 1, 1)
        hp[2] -= dot(vb[4 + m], col, 1, 1)

    send(always, msend.at[xo // 2], mrecv.at[x // 2], r_ms.at[x // 2], lambda: dev(xo, zh, c, y, zl))
    mrecv[x // 2] = msend[x // 2]

    for k in (6, 7):
        arrive(jnp.logical_not(mover) & jnp.logical_not(is_pd2), cb.at[k], r_cb.at[k])
        rows_here(k)

    for part, recv in pieces(l0i, r_l0):
        arrive(still & jnp.logical_not(root), part, recv)

    def last_panel(w, high, low):
        return solve_panel(hp[w] + high.astype(F32) + low.astype(F32), l0i[...])

    col = last_panel(2, cb[6], cb[7])
    col = jnp.where(t == 2, 0.0, col).astype(BF16)
    for r in range(2):
        tile = row_tiles[r]
        full = last_panel(r, rb[6, r, c], rb[7, r, c])
        full = jnp.where(lower | (tile != 2), full, 0.0).astype(BF16)
        root_out[r, 0] = dot(pick, full, 1, 0).astype(BF16)
        row = jnp.where(tile == 2, jnp.zeros_like(full), full)
        schur_out[r] = (acc[r] - dot(row, col, 1, 1)).astype(BF16)

    for s in range(4):
        arrive(x != s, precv.at[s], r_ps.at[s])
    for s in range(2):
        arrive(x // 2 != s, mrecv.at[s], r_ms.at[s])
    for s in range(4):
        for r in range(2):
            leaf_out[4 * r + s, 0] = precv[s, r].astype(BF16)
    for s in range(2):
        for r in range(2):
            mid_out[2 * r + s, 0] = mrecv[s, r].astype(BF16)

    def wait_all(entries):
        for pred, makers in entries:

            @pl.when(pred)
            def _(makers=makers):
                for make in makers:
                    make().wait_send()

    for outer, entries in pending.values():
        if outer is None:
            wait_all(entries)
        else:
            pl.when(outer)(lambda entries=entries: wait_all(entries))


def per_device(leaf, middle, root, s2, s1, o2, o1):
    vmem = pl.BlockSpec(memory_space=pltpu.VMEM)
    smem = pl.BlockSpec(memory_space=pltpu.SMEM)
    dma = pltpu.SemaphoreType.DMA
    outs = [
        jax.ShapeDtypeStruct((8, 1, 8, W), BF16),
        jax.ShapeDtypeStruct((4, 1, 8, W), BF16),
        jax.ShapeDtypeStruct((2, 1, 8, W), BF16),
        jax.ShapeDtypeStruct((2, W, W), BF16),
    ]
    tile = (W, W)
    scratch = [
        pltpu.VMEM((4, 2) + tile, F32),
        pltpu.VMEM((2, 2) + tile, F32),
        pltpu.VMEM(tile, F32),
        pltpu.VMEM((8,) + tile, BF16),
        pltpu.VMEM((8, 2, 2) + tile, BF16),
        pltpu.VMEM(tile, F32),
        pltpu.VMEM((2,) + tile, BF16),
        pltpu.VMEM(tile, F32),
        pltpu.VMEM(tile, F32),
        pltpu.VMEM(tile, F32),
        pltpu.VMEM((4, 3) + tile, BF16),
        pltpu.VMEM((2, 3) + tile, BF16),
        pltpu.VMEM((2,) + tile, F32),
        pltpu.VMEM((2,) + tile, F32),
        pltpu.VMEM((4, 2, 8, W), F32),
        pltpu.VMEM((4, 2, 8, W), F32),
        pltpu.VMEM((2, 2, 8, W), F32),
        pltpu.VMEM((2, 2, 8, W), F32),
        pltpu.VMEM((2, 2) + tile, F32),
        pltpu.VMEM((6,) + tile, BF16),
        pltpu.VMEM((3,) + tile, F32),
        pltpu.VMEM((2,) + tile, BF16),
        dma((SENDS,)),
        dma((4, 2)), dma((2, 2)), dma, dma((8,)), dma((8, 2, 2, 2)),
        dma((3,)), dma((2,)), dma((3,)), dma((3,)), dma((4,)), dma((2,)), dma((2, 2)), dma((6,)), dma((2,)),
    ]
    *panels, schur = pl.pallas_call(
        kernel,
        out_shape=outs,
        in_specs=[vmem] * 5 + [smem] * 2,
        out_specs=[vmem] * 4,
        scratch_shapes=scratch,
        compiler_params=pltpu.CompilerParams(has_side_effects=True, collective_id=0, vmem_limit_bytes=60 * 2**20),
        name="window",
    )(leaf.reshape(8, W, W), middle.reshape(4, W, W), root.reshape(2, W, W), s2, s1, o2, o1)
    return (*panels, schur.reshape(2, W, 1, W))


SENDS = 560


def solution(mesh):
    return jax.shard_map(
        per_device,
        mesh=mesh,
        in_specs=(P(None, "cube", None, "tile"),) * 3 + (P(),) * 4,
        out_specs=(P(None, "cube", "tile", None),) * 3 + (P(None, "cube", None, "tile"),),
        check_vma=False,
    )
```
